32 devices in a mesh: ctx: 16 (over z, y, core), head: 2 (over x).
Axes of the slice: x: 2, y: 2, z: 4, core: 2. Of those that a mesh axis runs over, the one named last changes fastest.
Arguments:
- queries: bfloat16 [16, 8192, 128], P('head', 'ctx'), may hold values from -20 to 20
- keys: bfloat16 [16, 8192, 128], P('head', 'ctx'), may hold values from -20 to 20
- values: bfloat16 [16, 8192, 128], P('head', 'ctx'), may hold values from -60 to 60
- out_grad: bfloat16 [16, 8192, 128], P('head', 'ctx'), may hold values from -6 to 6
- norm_gain: float32 [16, 128], P('head'), may hold values from 0.25 to 1.75
- doc_start: int32 [8192], replicated, may hold values from 0 to 1536, as said below
- head_offsets: int32 [16], P('head'), may hold values from 0 to 31
Outputs:
- normed: bfloat16 [16, 8192, 128], P('head', 'ctx')
- grad_queries: bfloat16 [16, 8192, 128], P('head', 'ctx')
- grad_keys: bfloat16 [16, 8192, 128], P('head', 'ctx')
- grad_values: bfloat16 [16, 8192, 128], P('head', 'ctx')
The draws below stay inside these ranges and needn't reach their ends.
Inputs may be any that keep to these rules, and one draw needn't show every extreme that they name: `doc_start`: each entry is the first position of its token's document: the token's own position or the previous token's entry; the window holds 4 documents, the last of which starts at (3) * 512.
All inputs are finite; a program needn't handle non-finite values.
Results may differ from the reference program's by a relative error of at most 0.023.
Values may be sent and summed in bfloat16 or wider, within the bound.
No kernel may reach another device: no remote copies, remote signals or barrier semaphores. Data moves between devices by JAX's collectives and lax.ppermute only.
A program may use at most 128 MiB of HBM per device.

```python
import math
import jax
import jax.numpy as jnp
from jax import lax

HEADS = 16
HD = 128
TOK_DEV = 512
SEL = 256
DOCS = 4
TOKENS = 8192
RATE = 32


def paired(key):
    shape = (HEADS, TOKENS, HD)
    query_field = jnp.clip(jax.random.normal(jax.random.fold_in(key, 104), shape, jnp.float32), -6.0, 6.0)
    key_field = jnp.clip(jax.random.normal(jax.random.fold_in(key, 105), shape, jnp.float32), -6.0, 6.0)
    return (jnp.clip(query_field, -20.0, 20.0), jnp.clip(key_field, -20.0, 20.0))


def draw_queries(key, part):
    return paired(key)[0].astype(jnp.bfloat16)


def draw_keys(key, part):
    return paired(key)[1].astype(jnp.bfloat16)


def draw_values(key, part):
    shape = (HEADS, TOKENS, HD)
    head_rank = jnp.arange(HEADS, dtype=jnp.float32)[:, None, None]
    jitter = jax.random.uniform(jax.random.fold_in(key, 201), (HEADS, 1, HD), jnp.float32)
    base = jnp.clip(jax.random.normal(jax.random.fold_in(key, 203), shape, jnp.float32), -4.0, 4.0)
    field = base * 10.0 ** ((head_rank + jitter) / HEADS)
    return jnp.clip(field, -60.0, 60.0).astype(jnp.bfloat16)


def draw_doc_start(key, part):
    span = TOKENS // 16
    jitter = jax.random.randint(jax.random.fold_in(key, 301), (DOCS - 1,), -(span // 4), span // 4 + 1)
    keep = (jnp.arange(DOCS - 1, dtype=jnp.int32) < DOCS - 2).astype(jnp.int32)
    cuts = jnp.arange(1, DOCS, dtype=jnp.int32) * span + jitter.astype(jnp.int32) * keep
    position = jnp.arange(TOKENS, dtype=jnp.int32)
    return jnp.max(jnp.where(position[:, None] >= cuts[None, :], cuts[None, :], 0), axis=1).astype(jnp.int32)


def with_ends(array, key, smallest, largest):
    longest = array.shape.index(max(array.shape))
    spots = []
    for shift in (0, 1):
        where = [jax.random.randint(jax.random.fold_in(key, axis), (), 0, length) for axis, length in enumerate(array.shape)]
        where[longest] = (where[longest] + shift) % array.shape[longest]
        spots.append(tuple(where))
    return array.at[spots[0]].set(smallest).at[spots[1]].set(largest)


def block_levels(own_key, shape, split, low, high):
    loudness = 1.0
    for axis_at, shards_of in split:
        steps = jax.random.uniform(jax.random.fold_in(jax.random.fold_in(own_key, 6), axis_at), (shards_of,), jnp.float32, low / len(split), high / len(split))
        loudness = loudness * jnp.repeat(jnp.exp(steps), shape[axis_at] // shards_of).reshape((-1,) + (1,) * (len(shape) - 1 - axis_at))
    return loudness


def centred(stream_key, extent, deviation, limit, split=(), kind=jnp.bfloat16):
    result = deviation * jax.random.normal(stream_key, extent, jnp.float32)
    if split:
        result = result * block_levels(stream_key, extent, split, -0.22, 0.18)
    return jnp.clip(result, -limit, limit).astype(kind)


def setup_inputs(seed: int = 0) -> dict:
    arg_keys = jax.random.split(jax.random.key(seed), 8)
    return {
        "queries": draw_queries(jax.random.fold_in(arg_keys[7], 71), 0),
        "keys": draw_keys(jax.random.fold_in(arg_keys[7], 71), 0),
        "values": draw_values(jax.random.fold_in(arg_keys[7], 71), 0),
        "out_grad": centred(arg_keys[3], (HEADS, TOKENS, HD), 1.0, 6.0, ((0, 2), (1, 16))),
        "norm_gain": jnp.clip(1.0 + 0.15 * jax.random.normal(arg_keys[4], (HEADS, HD), jnp.float32), 0.25, 1.75),
        "doc_start": draw_doc_start(jax.random.fold_in(arg_keys[7], 71), 0),
        "head_offsets": with_ends(jax.random.randint(arg_keys[6], (HEADS,), 0, RATE), jax.random.fold_in(arg_keys[6], 1), 0, RATE - 1).astype(jnp.int32),
    }


theta_base = 10000.0
eps_norm = 1e-06

def rotate(field, rel, sign):
    half = field.shape[-1] // 2
    freq = theta_base ** (-2.0 * jnp.arange(half).astype(rel.dtype) / field.shape[-1])
    angle = rel[:, None] * freq[None, :]
    cosine = jnp.cos(angle)
    sine = sign * jnp.sin(angle)
    first = field[..., :half]
    second = field[..., half:]
    return jnp.concatenate([first * cosine - second * sine, second * cosine + first * sine], axis=-1)

def rounded(field):
    return lax.optimization_barrier(field.astype(jnp.bfloat16))

def reference(queries, keys, values, out_grad, norm_gain, doc_start, head_offsets):
    f32 = jnp.float32
    scale = 1.0 / math.sqrt(HD)
    span = 2 * TOK_DEV
    segs = TOKENS // span
    groups = segs + 1
    position = jnp.arange(TOKENS, dtype=jnp.int32)
    rel = (position - doc_start).astype(f32)
    q_rot = rounded(rotate(queries.astype(f32), rel, 1.0))
    k_rot = rounded(rotate(keys.astype(f32), rel, 1.0))
    local = jnp.arange(span, dtype=jnp.int32)

    def view(field, lead):
        widths = [(0, 0), (lead, span - lead)] + [(0, 0)] * (field.ndim - 2)
        padded = jnp.pad(field, widths)
        return jnp.swapaxes(padded.reshape((field.shape[0], groups, span) + field.shape[2:]), 0, 1)

    def unview(field, lead):
        moved = jnp.swapaxes(field, 0, 1)
        moved = moved.reshape((moved.shape[0], groups * span) + moved.shape[3:])
        return moved[:, lead:lead + TOKENS]

    def alternate(even, odd):
        return jnp.stack([even, odd], axis=1).reshape((HEADS,) + even.shape[1:])

    def group_rows(phase):
        lead = phase * TOK_DEV
        start_seg = jnp.pad(doc_start, (lead, span - lead)).reshape(groups, span)
        base_seg = jnp.arange(groups, dtype=jnp.int32) * span - lead
        return (lead, start_seg, base_seg)

    def seg_scores(q_part, k_part, start_row, base):
        pos = base + local
        real = (pos >= 0) & (pos < TOKENS)
        causal = (local[None, :] <= local[:, None]) & (pos[None, :] >= start_row[:, None])
        diag = local[None, :] == local[:, None]
        valid = jnp.where(real[:, None], causal, diag)
        score = jnp.einsum('hid,hjd->hij', q_part.astype(f32), k_part.astype(f32)) * scale
        return jnp.where(valid[None], score, -jnp.inf)

    def seg_lse(item):
        return jax.nn.logsumexp(seg_scores(*item), axis=-1)
    lse_parts = []
    for phase in range(2):
        lead, start_seg, base_seg = group_rows(phase)
        part = lax.map(seg_lse, (view(q_rot[phase::2], lead), view(k_rot[phase::2], lead), start_seg, base_seg))
        lse_parts.append(unview(part, lead))
    lse0 = alternate(lse_parts[0], lse_parts[1])
    index = head_offsets[:, None] + RATE * jnp.arange(SEL, dtype=jnp.int32)[None, :]
    heads_idx = jnp.arange(HEADS, dtype=jnp.int32)[:, None]

    def pick(field):
        return jnp.take_along_axis(field, index[:, :, None], axis=1)
    q_one = pick(q_rot)
    k_one = pick(k_rot)
    v_one = pick(values)
    start_one = doc_start[index]
    order = jnp.arange(SEL, dtype=jnp.int32)
    mask_one = (order[None, None, :] <= order[None, :, None]) & (index[:, None, :] >= start_one[:, :, None])
    z_one = jnp.where(mask_one, jnp.einsum('hid,hjd->hij', q_one.astype(f32), k_one.astype(f32)) * scale, -jnp.inf)
    lse_one = jax.nn.logsumexp(z_one, axis=-1)
    lse_sel = jnp.logaddexp(jnp.take_along_axis(lse0, index, axis=1), lse_one)
    lse = lse0.at[heads_idx, index].set(lse_sel)
    p_one = rounded(jnp.exp(z_one - lse_sel[:, :, None])).astype(f32)
    o_one = jnp.einsum('hij,hjd->hid', p_one, v_one.astype(f32))

    def seg_out(item):
        q_part, k_part, v_part, start_row, base, lse_row = item
        score = seg_scores(q_part, k_part, start_row, base)
        prob = rounded(jnp.exp(score - lse_row[:, :, None])).astype(f32)
        return jnp.einsum('hij,hjd->hid', prob, v_part.astype(f32))
    out_parts = []
    for phase in range(2):
        lead, start_seg, base_seg = group_rows(phase)
        part = lax.map(seg_out, (view(q_rot[phase::2], lead), view(k_rot[phase::2], lead), view(values[phase::2], lead), start_seg, base_seg, view(lse[phase::2], lead)))
        out_parts.append(unview(part, lead))
    o_zero = alternate(out_parts[0], out_parts[1])
    attn = rounded(o_zero.at[heads_idx, index].add(o_one))
    attn_f = attn.astype(f32)
    feats = HEADS * HD
    rinv = lax.rsqrt(lax.optimization_barrier(jnp.sum(attn_f * attn_f, axis=(0, 2))) / feats + eps_norm)
    gain = norm_gain[:, None, :]
    normed = (attn_f * rinv[None, :, None] * gain).astype(jnp.bfloat16)
    scaled_grad = gain * out_grad.astype(f32)
    cstat = lax.optimization_barrier(jnp.sum(scaled_grad * attn_f, axis=(0, 2))) / feats
    attn_grad = rounded(rinv[None, :, None] * (scaled_grad - attn_f * (rinv * rinv * cstat)[None, :, None]))
    grad_f = attn_grad.astype(f32)
    delta = lax.optimization_barrier(jnp.sum(grad_f * attn_f, axis=2))
    half = TOK_DEV

    def split_sum(low, high):
        first = low[:, :half] + rounded(high[:, :half]).astype(f32)
        return jnp.concatenate([first, low[:, half:] + high[:, half:]], axis=1)

    def seg_back(item):
        q_part, k_part, v_part, start_row, base, lse_row, grad_row, delta_row = item
        score = seg_scores(q_part, k_part, start_row, base)
        prob = rounded(jnp.exp(score - lse_row[:, :, None])).astype(f32)
        grad_part = grad_row.astype(f32)
        q_full = q_part.astype(f32)
        dprob = jnp.einsum('hid,hjd->hij', grad_part, v_part.astype(f32))
        dscore = rounded(prob * (dprob - delta_row[:, :, None])).astype(f32)
        dq_part = jnp.einsum('hij,hjd->hid', dscore, k_part.astype(f32)) * scale
        dk_low = jnp.einsum('hij,hid->hjd', dscore[:, :half], q_full[:, :half]) * scale
        dk_high = jnp.einsum('hij,hid->hjd', dscore[:, half:], q_full[:, half:]) * scale
        dv_low = jnp.einsum('hij,hid->hjd', prob[:, :half], grad_part[:, :half])
        dv_high = jnp.einsum('hij,hid->hjd', prob[:, half:], grad_part[:, half:])
        return (dq_part, split_sum(dk_low, dk_high), split_sum(dv_low, dv_high))
    back_parts = []
    for phase in range(2):
        lead, start_seg, base_seg = group_rows(phase)
        dq_seg, dk_seg, dv_seg = lax.map(seg_back, (view(q_rot[phase::2], lead), view(k_rot[phase::2], lead), view(values[phase::2], lead), start_seg, base_seg, view(lse[phase::2], lead), view(attn_grad[phase::2], lead), view(delta[phase::2], lead)))
        back_parts.append((unview(dq_seg, lead), unview(dk_seg, lead), unview(dv_seg, lead)))
    dq = alternate(back_parts[0][0], back_parts[1][0])
    dk = alternate(back_parts[0][1], back_parts[1][1])
    dv = alternate(back_parts[0][2], back_parts[1][2])
    grad_one = pick(attn_grad).astype(f32)
    delta_one = jnp.take_along_axis(delta, index, axis=1)
    dprob_one = jnp.einsum('hid,hjd->hij', grad_one, v_one.astype(f32))
    dscore_one = rounded(p_one * (dprob_one - delta_one[:, :, None])).astype(f32)
    dq_one = jnp.einsum('hij,hjd->hid', dscore_one, k_one.astype(f32)) * scale
    dk_one = jnp.einsum('hij,hid->hjd', dscore_one, q_one.astype(f32)) * scale
    dv_one = jnp.einsum('hij,hid->hjd', p_one, grad_one)
    dq = dq.at[heads_idx, index].add(dq_one)
    dk = dk.at[heads_idx, index].add(dk_one)
    dv = dv.at[heads_idx, index].add(dv_one)
    grad_queries = rotate(dq, rel, -1.0).astype(jnp.bfloat16)
    grad_keys = rotate(dk, rel, -1.0).astype(jnp.bfloat16)
    grad_values = dv.astype(jnp.bfloat16)
    return (normed, grad_queries, grad_keys, grad_values)
```

```python
import math

import jax
import jax.numpy as jnp
from jax import lax
from jax.experimental import pallas as pl
from jax.experimental.pallas import tpu as pltpu
from jax.sharding import PartitionSpec as P

HEADS = 16
SEL = 256
theta_base = 10000.0
eps_norm = 1e-06
NEG = -1e30
f32 = jnp.float32
bf16 = jnp.bfloat16


def dot_nn(a, b):
    return lax.dot_general(a, b, (((1,), (0,)), ((), ())), preferred_element_type=f32)


def dot_nt(a, b):
    return lax.dot_general(a, b, (((1,), (1,)), ((), ())), preferred_element_type=f32)


def dot_tn(a, b):
    return lax.dot_general(a, b, (((0,), (0,)), ((), ())), preferred_element_type=f32)


def lanes_of(shape):
    return lax.broadcasted_iota(jnp.int32, shape, len(shape) - 1)


def rows_of(shape):
    return lax.broadcasted_iota(jnp.int32, shape, len(shape) - 2)


def low_half(x):
    return jnp.where(lanes_of(x.shape) < 64, x, pltpu.roll(x, 64, 1))


def high_half(x):
    return jnp.where(lanes_of(x.shape) < 64, pltpu.roll(x, 64, 1), x)


def unpack_tables(cos_ref, sin_ref):
    c, s = cos_ref[...], sin_ref[...]
    cos = jnp.concatenate([low_half(c), high_half(c)], axis=0)
    sin = jnp.concatenate([low_half(s), high_half(s)], axis=0)
    sin = jnp.where(lanes_of(sin.shape) < 64, -sin, sin)
    return cos, sin


def rot(x, cos, sin):
    return x * cos + pltpu.roll(x, 64, 1) * sin


def spread(row):
    parts = []
    for i in range(row.shape[0]):
        parts.append(jnp.broadcast_to(row[i : i + 1, :], (128, 128)).T)
    return jnp.concatenate(parts, axis=0)


def compact(x):
    eye = rows_of((128, 128)) == lanes_of((128, 128))
    parts = []
    for i in range(x.shape[0] // 128):
        block = x[i * 128 : (i + 1) * 128, :]
        parts.append(jnp.sum(jnp.where(eye, block, 0.0), axis=0, keepdims=True))
    return jnp.concatenate(parts, axis=0)


def row_sum(x):
    return jnp.broadcast_to(jnp.sum(x, axis=1, keepdims=True), x.shape)


def prep_kernel(info, offs, q_ref, k_ref, v_ref, cos_ref, sin_ref, qr_ref, kr_ref, send_ref, rows_ref):
    g = pl.program_id(0)
    par = info[1]
    tok = q_ref.shape[1]
    nb = rows_ref.shape[2]
    rate = tok // nb
    cos, sin = unpack_tables(cos_ref, sin_ref)
    for hh in range(2):
        off = offs[2 * g + hh]
        hot = (lanes_of((nb, tok)) == off + rate * rows_of((nb, tok))).astype(bf16)
        qr = rot(q_ref[hh].astype(f32), cos, sin).astype(bf16)
        kr = rot(k_ref[hh].astype(f32), cos, sin).astype(bf16)
        qr_ref[hh] = qr
        kr_ref[hh] = kr
        rows_ref[0, hh] = dot_nn(hot, kr).astype(bf16)
        rows_ref[1, hh] = dot_nn(hot, v_ref[hh]).astype(bf16)
        rows_ref[2, hh] = dot_nn(hot, qr).astype(bf16)
    send_ref[0, 0] = kr_ref[par]
    send_ref[1, 0] = v_ref[par]


def own_kernel(start_ref, q_ref, k_ref, v_ref, e_ref, acc_ref, ml_ref, bias_ref):
    tok = q_ref.shape[1]
    half = tok // 2
    scale = 1.0 / math.sqrt(q_ref.shape[2])

    @pl.when(pl.program_id(0) == 0)
    def _():
        start = spread(start_ref[...])
        for c in range(tok // 128):
            key = lanes_of((tok, 128)) + c * 128
            ok = (key <= rows_of((tok, 128))) & (key.astype(f32) >= start)
            bias_ref[:, c * 128 : (c + 1) * 128] = jnp.where(ok, 0.0, NEG)

    vals = jnp.concatenate([v_ref[0], jnp.ones((tok, 128), bf16)], axis=1)
    for c in range(2):
        lo, n = c * half, (c + 1) * half
        z = dot_nt(q_ref[0, lo : lo + half, :], k_ref[0, :n, :]) * scale + bias_ref[lo : lo + half, :n]
        m = jnp.max(z, axis=1, keepdims=True)
        e = jnp.exp(z - m).astype(bf16)
        e_ref[0, lo : lo + half, :n] = e
        out = dot_nn(e, vals[:n])
        acc_ref[0, lo : lo + half, :] = out[:, :128]
        mb = jnp.broadcast_to(m, (half, 128))
        ml_ref[0, lo : lo + half, :] = jnp.where(lanes_of((half, 128)) < 64, mb, out[:, 128:])


def key_order(index, codes, nb, part, count):
    col = lanes_of((1, count)) + part * count
    slot = col // nb
    dev = jnp.full((1, count), index, jnp.int32)
    for b, code in enumerate(codes):
        dev = dev ^ (((slot >> b) & 1) * code)
    return dev * nb + col % nb


def make_join_kernel(codes):
    def join_kernel(
        info, offs, start_ref, q_ref, kv_ref, acc_ref, ml_ref, rows_ref, ga_ref, gb_ref, og_ref, gain_ref,
        e_ref, attn_ref, rr_ref, e1_ref, rs_ref, ar_ref, or_ref, stat_ref,
        bias_ref, start_s, m_s, l_s, acc_s, mp_s, sq_s, cr_s,
    ):
        g = pl.program_id(0)
        index, par, sel = info[0], info[1], info[2]
        tok = q_ref.shape[1]
        nb = rows_ref.shape[2]
        rate = tok // nb
        half = tok // 2
        count = ga_ref.shape[2]
        scale = 1.0 / math.sqrt(q_ref.shape[2])

        @pl.when(g == 0)
        def _():
            start = spread(start_ref[...])
            start_s[...] = start
            first = jnp.where(index == 0, float(tok), 0.0)
            for c in range(tok // 128):
                key = (lanes_of((tok, 128)) + c * 128).astype(f32)
                ok = (key - tok >= start) & (key >= first)
                bias_ref[:, c * 128 : (c + 1) * 128] = jnp.where(ok, 0.0, NEG)
            sq_s[...] = jnp.zeros_like(sq_s)
            cr_s[...] = jnp.zeros_like(cr_s)

        vals = jnp.concatenate([kv_ref[1, 0], jnp.ones((tok, 128), bf16)], axis=1)
        for c in range(2):
            lo = c * half
            z = dot_nt(q_ref[sel, lo : lo + half, :], kv_ref[0, 0]) * scale + bias_ref[lo : lo + half, :]
            m = jnp.max(z, axis=1, keepdims=True)
            e = jnp.exp(z - m).astype(bf16)
            e_ref[0, lo : lo + half, :] = e
            out = dot_nn(e, vals)
            acc_s[lo : lo + half, :] = out[:, :128]
            l_s[lo : lo + half, :] = out[:, 128:]
            mp_s[lo : lo + half, :] = jnp.broadcast_to(m, (half, 128))

        for hh in range(2):
            off = offs[2 * g + hh]
            rows = pl.ds(off, nb, stride=rate)
            here = sel == hh
            ml = ml_ref[hh]
            m_own = low_half(ml)
            l_own = high_half(ml)
            m_prev = jnp.where(here, mp_s[...], NEG)
            m = jnp.maximum(m_own, m_prev)
            a_own = jnp.exp(m_own - m)
            a_prev = jnp.where(here, jnp.exp(m_prev - m), 0.0)
            m_s[...] = m
            lsum = a_own * l_own + a_prev * l_s[...]
            total = a_own * acc_ref[hh] + a_prev * acc_s[...]

            q1 = rows_ref[2, hh]
            start1 = start_s[rows, :][:, :1]
            qb = index * nb + rows_of((nb, count))
            zs = []
            for part, ref in enumerate((ga_ref, gb_ref)):
                kb = key_order(index, codes, nb, part, count)
                pos = (off + rate * kb - index * tok).astype(f32)
                ok = (kb <= qb) & (pos >= start1)
                zs.append(jnp.where(ok, dot_nt(q1, ref[0, hh]) * scale, NEG))
            m1 = jnp.maximum(jnp.max(zs[0], axis=1, keepdims=True), jnp.max(zs[1], axis=1, keepdims=True))
            o1 = jnp.zeros((nb, 256), f32)
            for part, ref in enumerate((ga_ref, gb_ref)):
                e1 = jnp.exp(zs[part] - m1).astype(bf16)
                e1_ref[hh, :, part * count : (part + 1) * count] = e1
                v1 = jnp.concatenate([ref[1, hh], jnp.ones((count, 128), bf16)], axis=1)
                o1 = o1 + dot_nn(e1, v1)

            keep_l = l_s[...]
            keep_acc = acc_s[...]
            l_s[...] = lsum
            acc_s[...] = total
            mr = m_s[rows, :]
            lr = l_s[rows, :]
            ar = acc_s[rows, :]
            m1b = jnp.broadcast_to(m1, (nb, 128))
            mn = jnp.maximum(mr, m1b)
            b0 = jnp.exp(mr - mn)
            b1 = jnp.exp(m1b - mn)
            ln = b0 * lr + b1 * o1[:, 128:]
            inv1 = 1.0 / ln
            m_s[rows, :] = mn
            l_s[rows, :] = ln
            acc_s[rows, :] = b0 * ar + b1 * o1[:, :128]
            lse1 = mn + jnp.log(ln)
            rs_ref[hh] = jnp.where(lanes_of((nb, 128)) < 64, lse1, b1 * inv1)

            m = m_s[...]
            inv = 1.0 / l_s[...]
            attn = (acc_s[...] * inv).astype(bf16)
            attn_ref[hh] = attn
            r_own = jnp.exp(m_own - m) * inv
            r_prev = jnp.where(here, jnp.exp(m_prev - m) * inv, 0.0)
            rr_ref[hh] = jnp.where(lanes_of((tok, 128)) < 64, r_own, r_prev)
            af = attn.astype(f32)
            gd = og_ref[hh].astype(f32) * gain_ref[hh]
            sq_s[...] += af * af
            cr_s[...] += gd * af
            hot = (lanes_of((nb, tok)) == off + rate * rows_of((nb, tok))).astype(bf16)
            ar_ref[hh] = dot_nn(hot, attn).astype(bf16)
            or_ref[hh] = dot_nn(hot, og_ref[hh]).astype(bf16)
            l_s[...] = keep_l
            acc_s[...] = keep_acc

        @pl.when(g == pl.num_programs(0) - 1)
        def _():
            stat_ref[...] = jnp.concatenate([compact(row_sum(sq_s[...])), compact(row_sum(cr_s[...]))], axis=0)

    return join_kernel


def norm_terms(stat_ref, other_ref, feats):
    total = stat_ref[...] + other_ref[...]
    n = total.shape[0] // 2
    rinv = lax.rsqrt(total[:n] / feats + eps_norm)
    return rinv, rinv * rinv * total[n:] / feats


def split3(x):
    hi = x.astype(bf16).astype(f32)
    mid = (x - hi).astype(bf16).astype(f32)
    return hi, mid, x - hi - mid


def make_rows_kernel(feats):
    def rows_kernel(offs, stat_ref, other_ref, ar_ref, or_ref, gain_ref, rs_ref, out_ref, rinv_s, cc_s):
        nb = ar_ref.shape[1]
        rate = rinv_s.shape[0] // nb
        rinv, cc = norm_terms(stat_ref, other_ref, feats)
        rinv_s[...] = spread(rinv)
        cc_s[...] = spread(cc)
        for h in range(ar_ref.shape[0]):
            rows = pl.ds(offs[h], nb, stride=rate)
            ri = rinv_s[rows, :]
            cr = cc_s[rows, :]
            af = ar_ref[h].astype(f32)
            gd = or_ref[h].astype(f32) * gain_ref[h]
            ag = (ri * (gd - af * cr)).astype(bf16)
            delta = row_sum(ag.astype(f32) * af)
            out_ref[0, h] = ag
            lane = lanes_of((nb, 128))
            pack = jnp.zeros((nb, 128), f32)
            for i, x in enumerate(split3(low_half(rs_ref[h])) + split3(delta)):
                pack = jnp.where(lane == i, x, pack)
            out_ref[1, h] = pack.astype(bf16)

    return rows_kernel


def grad_terms(attn_ref, og_ref, gain_ref, rinv_s, cc_s):
    af = attn_ref[0].astype(f32)
    gd = og_ref[0].astype(f32) * gain_ref[0]
    rinv = rinv_s[...]
    ag = (rinv * (gd - af * cc_s[...])).astype(bf16).astype(f32)
    delta = row_sum(ag * af)
    return af, rinv, ag, delta


def make_back_prev_kernel(feats):
    def back_prev_kernel(
        info, stat_ref, other_ref, q_ref, attn_ref, og_ref, gain_ref, rr_ref, kv_ref, e_ref,
        back_ref, dq_ref, rinv_s, cc_s,
    ):
        tok = q_ref.shape[1]
        half = tok // 2
        scale = 1.0 / math.sqrt(q_ref.shape[2])

        @pl.when(pl.program_id(0) == 0)
        def _():
            rinv, cc = norm_terms(stat_ref, other_ref, feats)
            rinv_s[...] = spread(rinv)
            cc_s[...] = spread(cc)

        af, rinv, ag, delta = grad_terms(attn_ref, og_ref, gain_ref, rinv_s, cc_s)
        r = high_half(rr_ref[0])
        do = (ag * r).astype(bf16)
        dl = delta * r
        dk = jnp.zeros((128, tok), f32)
        dv = jnp.zeros((128, tok), f32)
        for c in range(2):
            sl = slice(c * half, (c + 1) * half)
            e = e_ref[0, sl, :]
            dp = dot_nt(do[sl], kv_ref[1, 0])
            ds = (e.astype(f32) * (dp - jnp.concatenate([dl[sl]] * (tok // 128), axis=1))).astype(bf16)
            dq_ref[0, sl, :] = dot_nn(ds, kv_ref[0, 0])
            dk = dk + dot_tn(q_ref[0, sl, :], ds)
            dv = dv + dot_tn(do[sl], e)
        back_ref[0, 0] = (dk * scale).T.astype(bf16)
        back_ref[1, 0] = dv.T.astype(bf16)

    return back_prev_kernel


def make_back_own_kernel(feats):
    def back_own_kernel(
        info, offs, stat_ref, other_ref, q_ref, k_ref, v_ref, attn_ref, og_ref, gain_ref, rr_ref, e_ref,
        dqp_ref, e1_ref, rs_ref, ga_ref, gb_ref, cos_ref, sin_ref,
        normed_ref, gq_ref, dk_ref, dv_ref, rinv_s, cc_s, ag_s, de_s, dq_s,
    ):
        h = pl.program_id(0)
        sel = info[2]
        tok = q_ref.shape[1]
        nb = e1_ref.shape[1]
        rate = tok // nb
        count = ga_ref.shape[2]
        half = tok // 2
        scale = 1.0 / math.sqrt(q_ref.shape[2])

        @pl.when(h == 0)
        def _():
            rinv, cc = norm_terms(stat_ref, other_ref, feats)
            rinv_s[...] = spread(rinv)
            cc_s[...] = spread(cc)

        af, rinv, ag, delta = grad_terms(attn_ref, og_ref, gain_ref, rinv_s, cc_s)
        normed_ref[0] = (af * rinv * gain_ref[0]).astype(bf16)
        ag_s[...] = ag
        de_s[...] = delta
        r = low_half(rr_ref[0])
        do = (ag * r).astype(bf16)
        dl = delta * r
        here = jnp.where(h % 2 == sel, 1.0, 0.0)
        dks = []
        for c in range(2):
            lo, n = c * half, (c + 1) * half
            sl = slice(lo, n)
            e = e_ref[0, sl, :n]
            dp = dot_nt(do[sl], v_ref[0, :n, :])
            ds = (e.astype(f32) * (dp - jnp.concatenate([dl[sl]] * (n // 128), axis=1))).astype(bf16)
            dq_s[sl, :] = dot_nn(ds, k_ref[0, :n, :]) + dqp_ref[0, sl, :] * here
            dks.append((dot_tn(q_ref[0, sl, :], ds), dot_tn(do[sl], e)))
        for i, ref in enumerate((dk_ref, dv_ref)):
            ref[0, :half, :] = (dks[0][i] + dks[1][i][:, :half]).T
            ref[0, half:, :] = dks[1][i][:, half:].T

        rows = pl.ds(offs[h], nb, stride=rate)
        r1 = high_half(rs_ref[0])
        g1 = (ag_s[rows, :] * r1).astype(bf16)
        d1 = (de_s[rows, :] * r1)[:, :1]
        dq1 = jnp.zeros((nb, 128), f32)
        for part, ref in enumerate((ga_ref, gb_ref)):
            dp1 = dot_nt(g1, ref[1, 0])
            ds1 = (e1_ref[0, :, part * count : (part + 1) * count].astype(f32) * (dp1 - d1)).astype(bf16)
            dq1 = dq1 + dot_nn(ds1, ref[0, 0])
        dq_s[rows, :] += dq1
        cos, sin = unpack_tables(cos_ref, sin_ref)
        gq_ref[0] = rot(dq_s[...] * scale, cos, -sin).astype(bf16)

    return back_own_kernel


def make_final_kernel(codes):
    def final_kernel(
        info, offs, start_ref, dk_ref, dv_ref, back_ref, rows_ref, ga_ref, gb_ref, sa_ref, sb_ref, cos_ref, sin_ref,
        gk_ref, gv_ref, dk_s, dv_s,
    ):
        h = pl.program_id(0)
        index, par = info[0], info[1]
        tok = dk_ref.shape[1]
        nb = rows_ref.shape[2]
        rate = tok // nb
        count = ga_ref.shape[2]
        scale = 1.0 / math.sqrt(dk_ref.shape[2])
        off = offs[h]
        here = (h % 2 == par) & (index < info[3] - 1)
        back = jnp.where(here, back_ref[0, 0].astype(f32), 0.0)
        dk_s[...] = dk_ref[0] * scale + back
        dv_s[...] = dv_ref[0] + jnp.where(here, back_ref[1, 0].astype(f32), 0.0)

        k1 = rows_ref[0, 0]
        v1 = rows_ref[1, 0]
        kb = index * nb + rows_of((nb, count))
        kpos = off + rate * kb
        pick = (rows_of((16, 128)) == lanes_of((16, 128))).astype(bf16)
        dk1 = jnp.zeros((nb, 128), f32)
        dv1 = jnp.zeros((nb, 128), f32)
        for part, (g, s) in enumerate(((ga_ref, sa_ref), (gb_ref, sb_ref))):
            qb = key_order(index, codes, nb, part, count)
            start = start_ref[0, part : part + 1, :]
            st = dot_nt(pick, s[1, 0])
            lse = st[0:1] + st[1:2] + st[2:3]
            delta = st[3:4] + st[4:5] + st[5:6]
            ok = (kb <= qb) & (kpos >= start)
            z = jnp.where(ok, dot_nt(k1, g[0, 0]) * scale - lse, NEG)
            p = jnp.exp(z).astype(bf16)
            dp = dot_nt(v1, s[0, 0])
            ds = (p.astype(f32) * (dp - delta)).astype(bf16)
            dk1 = dk1 + dot_nn(ds, g[0, 0])
            dv1 = dv1 + dot_nn(p, s[0, 0])
        rows = pl.ds(off, nb, stride=rate)
        dk_s[rows, :] += dk1 * scale
        dv_s[rows, :] += dv1
        cos, sin = unpack_tables(cos_ref, sin_ref)
        gk_ref[0] = rot(dk_s[...], cos, -sin).astype(bf16)
        gv_ref[0] = dv_s[...].astype(bf16)

    return final_kernel


def call(kernel, prefetch, grid, ins, outs, scratch=()):
    arrays = [a for a, _, _ in ins]
    in_specs = [pl.BlockSpec(b, m) for _, b, m in ins]
    return pl.pallas_call(
        kernel,
        out_shape=[jax.ShapeDtypeStruct(s, d) for s, d, _, _ in outs],
        grid_spec=pltpu.PrefetchScalarGridSpec(
            num_scalar_prefetch=len(prefetch),
            grid=grid,
            in_specs=in_specs,
            out_specs=[pl.BlockSpec(b, m) for _, _, b, m in outs],
            scratch_shapes=list(scratch),
        ),
        compiler_params=pltpu.CompilerParams(
            dimension_semantics=("arbitrary",) * len(grid), vmem_limit_bytes=56 << 20
        ),
    )(*prefetch, *arrays)


def body(queries, keys, values, out_grad, norm_gain, doc_start, head_offsets):
    heads, tok, width = queries.shape
    ctx = lax.axis_size("ctx")
    rate = ctx * tok // SEL
    nb = tok // rate
    feats = float(HEADS * width)
    pairs = heads // 2
    index = lax.axis_index("ctx")
    base = index * tok
    codes = [1 << b for b in range(1, ctx.bit_length() - 1)] + [1]

    starts = lax.dynamic_slice_in_dim(doc_start, base, tok)
    position = base + jnp.arange(tok, dtype=jnp.int32)
    rel = (position - starts).astype(f32)
    freq = theta_base ** (-2.0 * jnp.arange(width // 2).astype(f32) / width)
    angle = jnp.concatenate([rel[: tok // 2, None] * freq[None, :], rel[tok // 2 :, None] * freq[None, :]], axis=1)
    cos, sin = jnp.cos(angle), jnp.sin(angle)
    start_rel = (starts - base).astype(f32).reshape(tok // 128, 128)
    info = jnp.stack([index, index % 2, (index + 1) % 2, jnp.int32(ctx)]).astype(jnp.int32)
    gain = norm_gain.reshape(heads, 1, width)

    sp = (tok // 128, 128)
    tab = (tok // 2, 128)
    pair3 = (2, tok, width)
    one3 = (1, tok, width)

    def const(n):
        return lambda i, *s: (0,) * n

    q_rot, k_rot, send, rows = call(
        prep_kernel, (info, head_offsets), (pairs,),
        [
            (queries, pair3, lambda g, *s: (g, 0, 0)),
            (keys, pair3, lambda g, *s: (g, 0, 0)),
            (values, pair3, lambda g, *s: (g, 0, 0)),
            (cos, tab, const(2)),
            (sin, tab, const(2)),
        ],
        [
            (queries.shape, bf16, pair3, lambda g, *s: (g, 0, 0)),
            (queries.shape, bf16, pair3, lambda g, *s: (g, 0, 0)),
            ((2, pairs, tok, width), bf16, (2, 1, tok, width), lambda g, *s: (0, g, 0, 0)),
            ((3, heads, nb, width), bf16, (3, 2, nb, width), lambda g, *s: (0, g, 0, 0)),
        ],
    )
    recv = lax.ppermute(send, "ctx", [(i, i + 1) for i in range(ctx - 1)])

    def exchange(x):
        for code in codes[:-1]:
            x = jnp.concatenate([x, lax.ppermute(x, "ctx", [(i, i ^ code) for i in range(ctx)])], axis=2)
        return x, lax.ppermute(x, "ctx", [(i, i ^ codes[-1]) for i in range(ctx)])

    ga, gb = exchange(rows)
    half_count = SEL // 2

    e_own, acc_own, ml_own = call(
        own_kernel, (), (heads,),
        [
            (start_rel, sp, const(2)),
            (q_rot, one3, lambda h, *s: (h, 0, 0)),
            (k_rot, one3, lambda h, *s: (h, 0, 0)),
            (values, one3, lambda h, *s: (h, 0, 0)),
        ],
        [
            ((heads, tok, tok), bf16, (1, tok, tok), lambda h, *s: (h, 0, 0)),
            (queries.shape, f32, one3, lambda h, *s: (h, 0, 0)),
            (queries.shape, f32, one3, lambda h, *s: (h, 0, 0)),
        ],
        [pltpu.VMEM((tok, tok), f32)],
    )

    g4 = lambda g, *s: (0, g, 0, 0)
    gp = lambda g, *s: (g, 0, 0)
    e_prev, attn, rr, e1, rs, attn_rows, og_rows, stat = call(
        make_join_kernel(codes), (info, head_offsets), (pairs,),
        [
            (start_rel, sp, const(2)),
            (q_rot, pair3, gp),
            (recv, (2, 1, tok, width), g4),
            (acc_own, pair3, gp),
            (ml_own, pair3, gp),
            (rows, (3, 2, nb, width), g4),
            (ga, (3, 2, half_count, width), g4),
            (gb, (3, 2, half_count, width), g4),
            (out_grad, pair3, gp),
            (gain, (2, 1, width), gp),
        ],
        [
            ((pairs, tok, tok), bf16, (1, tok, tok), gp),
            (queries.shape, bf16, pair3, gp),
            (queries.shape, f32, pair3, gp),
            ((heads, nb, SEL), bf16, (2, nb, SEL), gp),
            ((heads, nb, width), f32, (2, nb, width), gp),
            ((heads, nb, width), bf16, (2, nb, width), gp),
            ((heads, nb, width), bf16, (2, nb, width), gp),
            ((2 * tok // 128, 128), f32, (2 * tok // 128, 128), const(2)),
        ],
        [pltpu.VMEM((tok, tok), f32)] + [pltpu.VMEM((tok, 128), f32)] * 7,
    )
    other = lax.ppermute(stat, "head", [(0, 1), (1, 0)])

    whole = lambda a: (a, a.shape, const(a.ndim))
    (grad_rows,) = call(
        make_rows_kernel(feats), (head_offsets,), (1,),
        [whole(stat), whole(other), whole(attn_rows), whole(og_rows), whole(gain), whole(rs)],
        [((2, heads, nb, width), bf16, (2, heads, nb, width), const(4))],
        [pltpu.VMEM((tok, 128), f32)] * 2,
    )
    sa, sb = exchange(grad_rows)

    gsel = lambda g, s, *_: (2 * g + s[2], 0, 0)
    back, dq_prev = call(
        make_back_prev_kernel(feats), (info,), (pairs,),
        [
            whole(stat), whole(other),
            (q_rot, one3, gsel),
            (attn, one3, gsel),
            (out_grad, one3, gsel),
            (gain, (1, 1, width), gsel),
            (rr, one3, gsel),
            (recv, (2, 1, tok, width), g4),
            (e_prev, (1, tok, tok), gp),
        ],
        [
            ((2, pairs, tok, width), bf16, (2, 1, tok, width), g4),
            ((pairs, tok, width), f32, one3, gp),
        ],
        [pltpu.VMEM((tok, 128), f32)] * 2,
    )
    back = lax.ppermute(back, "ctx", [(i + 1, i) for i in range(ctx - 1)])

    hp = lambda h, *s: (h, 0, 0)
    hg = lambda h, *s: (0, h, 0, 0)
    normed, grad_queries, dk_own, dv_own = call(
        make_back_own_kernel(feats), (info, head_offsets), (heads,),
        [
            whole(stat), whole(other),
            (q_rot, one3, hp),
            (k_rot, one3, hp),
            (values, one3, hp),
            (attn, one3, hp),
            (out_grad, one3, hp),
            (gain, (1, 1, width), hp),
            (rr, one3, hp),
            (e_own, (1, tok, tok), hp),
            (dq_prev, one3, lambda h, *s: (h // 2, 0, 0)),
            (e1, (1, nb, SEL), hp),
            (rs, (1, nb, width), hp),
            (ga, (2, 1, half_count, width), hg),
            (gb, (2, 1, half_count, width), hg),
            whole(cos), whole(sin),
        ],
        [
            (queries.shape, bf16, one3, hp),
            (queries.shape, bf16, one3, hp),
            (queries.shape, f32, one3, hp),
            (queries.shape, f32, one3, hp),
        ],
        [pltpu.VMEM((tok, 128), f32)] * 5,
    )

    slot = jnp.arange(ctx, dtype=jnp.int32)
    dev = jnp.full((ctx,), index, jnp.int32)
    for b, code in enumerate(codes):
        dev = dev ^ (((slot >> b) & 1) * code)
    qb = (dev[:, None] * nb + jnp.arange(nb, dtype=jnp.int32)[None, :]).reshape(-1)
    query_pos = head_offsets[:, None] + rate * qb[None, :]
    query_start = jnp.take(doc_start, query_pos).reshape(heads, 2, half_count)

    grad_keys, grad_values = call(
        make_final_kernel(codes), (info, head_offsets), (heads,),
        [
            (query_start, (1, 2, half_count), hp),
            (dk_own, one3, hp),
            (dv_own, one3, hp),
            (back, (2, 1, tok, width), lambda h, *s: (0, h // 2, 0, 0)),
            (rows, (2, 1, nb, width), hg),
            (ga, (1, 1, half_count, width), lambda h, *s: (2, h, 0, 0)),
            (gb, (1, 1, half_count, width), lambda h, *s: (2, h, 0, 0)),
            (sa, (2, 1, half_count, width), hg),
            (sb, (2, 1, half_count, width), hg),
            whole(cos), whole(sin),
        ],
        [
            (queries.shape, bf16, one3, hp),
            (queries.shape, bf16, one3, hp),
        ],
        [pltpu.VMEM((tok, 128), f32)] * 2,
    )
    return (normed, grad_queries, grad_keys, grad_values)


def solution(mesh):
    return jax.shard_map(
        body,
        mesh=mesh,
        in_specs=(
            P("head", "ctx", None),
            P("head", "ctx", None),
            P("head", "ctx", None),
            P("head", "ctx", None),
            P("head", None),
            P(),
            P("head"),
        ),
        out_specs=(
            P("head", "ctx", None),
            P("head", "ctx", None),
            P("head", "ctx", None),
            P("head", "ctx", None),
        ),
        check_vma=False,
    )
```

```python
import math

import jax
import jax.numpy as jnp
from jax import lax
from jax.experimental import pallas as pl
from jax.experimental.pallas import tpu as pltpu
from jax.sharding import PartitionSpec as P

HEADS = 16
SEL = 256
theta_base = 10000.0
eps_norm = 1e-06
NEG = -1e30
f32 = jnp.float32
bf16 = jnp.bfloat16


def dot_nn(a, b):
    return lax.dot_general(a, b, (((1,), (0,)), ((), ())), preferred_element_type=f32)


def dot_nt(a, b):
    return lax.dot_general(a, b, (((1,), (1,)), ((), ())), preferred_element_type=f32)


def dot_tn(a, b):
    return lax.dot_general(a, b, (((0,), (0,)), ((), ())), preferred_element_type=f32)


def lanes_of(shape):
    return lax.broadcasted_iota(jnp.int32, shape, len(shape) - 1)


def rows_of(shape):
    return lax.broadcasted_iota(jnp.int32, shape, len(shape) - 2)


def low_half(x):
    return jnp.where(lanes_of(x.shape) < 64, x, pltpu.roll(x, 64, 1))


def high_half(x):
    return jnp.where(lanes_of(x.shape) < 64, pltpu.roll(x, 64, 1), x)


def unpack_tables(cos_ref, sin_ref):
    c, s = cos_ref[...], sin_ref[...]
    cos = jnp.concatenate([low_half(c), high_half(c)], axis=0)
    sin = jnp.concatenate([low_half(s), high_half(s)], axis=0)
    sin = jnp.where(lanes_of(sin.shape) < 64, -sin, sin)
    return cos, sin


def rot(x, cos, sin):
    return x * cos + pltpu.roll(x, 64, 1) * sin


def spread(row):
    parts = []
    for i in range(row.shape[0]):
        parts.append(jnp.broadcast_to(row[i : i + 1, :], (128, 128)).T)
    return jnp.concatenate(parts, axis=0)


def compact(x):
    eye = rows_of((128, 128)) == lanes_of((128, 128))
    parts = []
    for i in range(x.shape[0] // 128):
        block = x[i * 128 : (i + 1) * 128, :]
        parts.append(jnp.sum(jnp.where(eye, block, 0.0), axis=0, keepdims=True))
    return jnp.concatenate(parts, axis=0)


def row_sum(x):
    return jnp.broadcast_to(jnp.sum(x, axis=1, keepdims=True), x.shape)


def prep_kernel(info, offs, k_ref, v_ref, cos_ref, sin_ref, kr_ref, vv_ref, send_ref, rows_ref):
    g = pl.program_id(0)
    par = info[1]
    tok = k_ref.shape[1]
    nb = rows_ref.shape[2]
    rate = tok // nb
    cos, sin = unpack_tables(cos_ref, sin_ref)
    for hh in range(2):
        h = 2 * g + hh
        hot = (lanes_of((nb, tok)) == offs[h] + rate * rows_of((nb, tok))).astype(bf16)
        kr = rot(k_ref[hh].astype(f32), cos, sin).astype(bf16)
        kr_ref[h] = kr
        vv_ref[h] = v_ref[hh]
        rows_ref[0, hh] = dot_nn(hot, kr).astype(bf16)
        rows_ref[1, hh] = dot_nn(hot, v_ref[hh]).astype(bf16)
    send_ref[0, 0] = kr_ref[2 * g + par]
    send_ref[1, 0] = v_ref[par]


def make_own_kernel(first, aliased):
    def own_kernel(info, offs, start_ref, q_ref, k_ref, v_ref, cos_ref, sin_ref, *refs):
        refs = refs[aliased:]
        qr_ref, e_ref, acc_ref, m_ref, l_ref, rows_ref, bias_ref = refs
        tok = q_ref.shape[1]
        nb = rows_ref.shape[1]
        rate = tok // nb
        half = tok // 2
        scale = 1.0 / math.sqrt(q_ref.shape[2])

        @pl.when(pl.program_id(0) == 0)
        def _():
            start = spread(start_ref[...])
            for c in range(tok // 128):
                key = lanes_of((tok, 128)) + c * 128
                ok = (key <= rows_of((tok, 128))) & (key.astype(f32) >= start)
                bias_ref[:, c * 128 : (c + 1) * 128] = jnp.where(ok, 0.0, NEG)

        cos, sin = unpack_tables(cos_ref, sin_ref)
        for hh in range(2):
            h = 2 * (pl.program_id(0) + first) + hh
            q = rot(q_ref[hh].astype(f32), cos, sin).astype(bf16)
            qr_ref[h] = q
            hot = (lanes_of((nb, tok)) == offs[h] + rate * rows_of((nb, tok))).astype(bf16)
            rows_ref[hh] = dot_nn(hot, q).astype(bf16)
            vals = jnp.concatenate([v_ref[h], jnp.ones((tok, 128), bf16)], axis=1)
            for c in range(2):
                lo, n = c * half, (c + 1) * half
                z = dot_nt(q[lo:n], k_ref[h, :n, :]) * scale + bias_ref[lo:n, :n]
                m = jnp.max(z, axis=1, keepdims=True)
                e = jnp.exp(z - m).astype(bf16)
                e_ref[h, lo:n, :n] = e
                out = dot_nn(e, vals[:n])
                acc_ref[h, lo:n, :] = out[:, :128]
                l_ref[h, lo:n, :] = out[:, 128:]
                m_ref[h, lo:n, :] = jnp.broadcast_to(m, (half, 128))

    return own_kernel


def prev_kernel(info, start_ref, q_ref, kv_ref, acc_in, m_ref, l_in, acc_ref, l_ref, mn_ref, e_ref, mp_ref, bias_ref):
    g = pl.program_id(0)
    index, sel = info[0], info[2]
    tok = q_ref.shape[1]
    half = tok // 2
    scale = 1.0 / math.sqrt(q_ref.shape[2])
    h = 2 * g + sel

    @pl.when(g == 0)
    def _():
        start = spread(start_ref[...])
        first = jnp.where(index == 0, float(tok), 0.0)
        for c in range(tok // 128):
            key = (lanes_of((tok, 128)) + c * 128).astype(f32)
            ok = (key - tok >= start) & (key >= first)
            bias_ref[:, c * 128 : (c + 1) * 128] = jnp.where(ok, 0.0, NEG)

    vals = jnp.concatenate([kv_ref[1, 0], jnp.ones((tok, 128), bf16)], axis=1)
    for c in range(2):
        sl = slice(c * half, (c + 1) * half)
        z = dot_nt(q_ref[h, sl, :], kv_ref[0, 0]) * scale + bias_ref[sl, :]
        m = jnp.max(z, axis=1, keepdims=True)
        e = jnp.exp(z - m).astype(bf16)
        e_ref[g, sl, :] = e
        out = dot_nn(e, vals)
        m_prev = jnp.broadcast_to(m, (half, 128))
        m_own = m_ref[h, sl, :]
        mn = jnp.maximum(m_own, m_prev)
        a_own = jnp.exp(m_own - mn)
        a_prev = jnp.exp(m_prev - mn)
        mp_ref[g, sl, :] = m_prev
        mn_ref[g, sl, :] = mn
        acc_ref[h, sl, :] = a_own * acc_in[h, sl, :] + a_prev * out[:, :128]
        l_ref[h, sl, :] = a_own * l_in[h, sl, :] + a_prev * out[:, 128:]


def key_order(index, codes, nb, part, count):
    col = lanes_of((1, count)) + part * count
    slot = col // nb
    dev = jnp.full((1, count), index, jnp.int32)
    for b, code in enumerate(codes):
        dev = dev ^ (((slot >> b) & 1) * code)
    return dev * nb + col % nb


def make_join_kernel(codes):
    def join_kernel(
        info, offs, start_ref, acc_ref, m_ref, l_ref, mn_ref, mp_ref, q1_ref, ga_ref, gb_ref, og_ref, gain_ref,
        attn_ref, rr_ref, e1_ref, rs_ref, ar_ref, or_ref, stat_ref,
        start_s, m_s, l_s, acc_s, sq_s, cr_s,
    ):
        g = pl.program_id(0)
        index, sel = info[0], info[2]
        tok = og_ref.shape[1]
        nb = q1_ref.shape[1]
        rate = tok // nb
        count = ga_ref.shape[2]
        scale = 1.0 / math.sqrt(og_ref.shape[2])

        @pl.when(g == 0)
        def _():
            start_s[...] = spread(start_ref[...])
            sq_s[...] = jnp.zeros_like(sq_s)
            cr_s[...] = jnp.zeros_like(cr_s)

        for hh in range(2):
            h = 2 * g + hh
            off = offs[h]
            rows = pl.ds(off, nb, stride=rate)
            here = sel == hh
            m_own = m_ref[h]
            m0 = jnp.where(here, mn_ref[g], m_own)
            m_s[hh] = m0
            l_s[hh] = l_ref[h]
            acc_s[hh] = acc_ref[h]

            q1 = q1_ref[hh]
            start1 = start_s[rows, :][:, :1]
            qb = index * nb + rows_of((nb, count))
            zs = []
            for part, ref in enumerate((ga_ref, gb_ref)):
                kb = key_order(index, codes, nb, part, count)
                pos = (off + rate * kb - index * tok).astype(f32)
                ok = (kb <= qb) & (pos >= start1)
                zs.append(jnp.where(ok, dot_nt(q1, ref[0, hh]) * scale, NEG))
            m1 = jnp.maximum(jnp.max(zs[0], axis=1, keepdims=True), jnp.max(zs[1], axis=1, keepdims=True))
            o1 = jnp.zeros((nb, 256), f32)
            for part, ref in enumerate((ga_ref, gb_ref)):
                e1 = jnp.exp(zs[part] - m1).astype(bf16)
                e1_ref[hh, :, part * count : (part + 1) * count] = e1
                v1 = jnp.concatenate([ref[1, hh], jnp.ones((count, 128), bf16)], axis=1)
                o1 = o1 + dot_nn(e1, v1)

            mr = m_s[hh, rows, :]
            lr = l_s[hh, rows, :]
            ar = acc_s[hh, rows, :]
            m1b = jnp.broadcast_to(m1, (nb, 128))
            mn = jnp.maximum(mr, m1b)
            b0 = jnp.exp(mr - mn)
            b1 = jnp.exp(m1b - mn)
            ln = b0 * lr + b1 * o1[:, 128:]
            m_s[hh, rows, :] = mn
            l_s[hh, rows, :] = ln
            acc_s[hh, rows, :] = b0 * ar + b1 * o1[:, :128]
            lse1 = mn + jnp.log(ln)
            rs_ref[hh] = jnp.where(lanes_of((nb, 128)) < 64, lse1, b1 / ln)

            inv = 1.0 / l_s[hh]
            attn = (acc_s[hh] * inv).astype(bf16)
            attn_ref[h] = attn
            both = jnp.where((lanes_of((tok, 128)) < 64) | jnp.logical_not(here), m_own, mp_ref[g])
            rr_ref[h] = jnp.exp(both - m_s[hh]) * inv
            af = attn.astype(f32)
            gd = og_ref[hh].astype(f32) * gain_ref[hh]
            sq_s[...] += af * af
            cr_s[...] += gd * af
            hot = (lanes_of((nb, tok)) == off + rate * rows_of((nb, tok))).astype(bf16)
            ar_ref[hh] = dot_nn(hot, attn).astype(bf16)
            or_ref[hh] = dot_nn(hot, og_ref[hh]).astype(bf16)

        @pl.when(g == pl.num_programs(0) - 1)
        def _():
            stat_ref[...] = jnp.concatenate([compact(row_sum(sq_s[...])), compact(row_sum(cr_s[...]))], axis=0)

    return join_kernel


def norm_terms(stat_ref, other_ref, feats):
    total = stat_ref[...] + other_ref[...]
    n = total.shape[0] // 2
    rinv = lax.rsqrt(total[:n] / feats + eps_norm)
    return rinv, rinv * rinv * total[n:] / feats


def split3(x):
    hi = x.astype(bf16).astype(f32)
    mid = (x - hi).astype(bf16).astype(f32)
    return hi, mid, x - hi - mid


def split3(x):
    hi = x.astype(bf16).astype(f32)
    mid = (x - hi).astype(bf16).astype(f32)
    return hi, mid, x - hi - mid


def split3(x):
    hi = x.astype(bf16).astype(f32)
    mid = (x - hi).astype(bf16).astype(f32)
    return hi, mid, x - hi - mid


def split3(x):
    hi = x.astype(bf16).astype(f32)
    mid = (x - hi).astype(bf16).astype(f32)
    return hi, mid, x - hi - mid


def split3(x):
    hi = x.astype(bf16).astype(f32)
    mid = (x - hi).astype(bf16).astype(f32)
    return hi, mid, x - hi - mid


def split3(x):
    hi = x.astype(bf16).astype(f32)
    mid = (x - hi).astype(bf16).astype(f32)
    return hi, mid, x - hi - mid


def split3(x):
    hi = x.astype(bf16).astype(f32)
    mid = (x - hi).astype(bf16).astype(f32)
    return hi, mid, x - hi - mid


def split3(x):
    hi = x.astype(bf16).astype(f32)
    mid = (x - hi).astype(bf16).astype(f32)
    return hi, mid, x - hi - mid


def make_rows_kernel(feats):
    def rows_kernel(offs, begin_ref, stat_ref, other_ref, ar_ref, or_ref, q1_ref, gain_ref, rs_ref, out_ref, rinv_s, cc_s, st_s):
        nb = ar_ref.shape[1]
        rate = rinv_s.shape[0] // nb
        rinv, cc = norm_terms(stat_ref, other_ref, feats)
        rinv_s[...] = spread(rinv)
        cc_s[...] = spread(cc)
        st_s[...] = spread(begin_ref[...])
        for h in range(ar_ref.shape[0]):
            rows = pl.ds(offs[h], nb, stride=rate)
            af = ar_ref[h].astype(f32)
            gd = or_ref[h].astype(f32) * gain_ref[h]
            ag = (rinv_s[rows, :] * (gd - af * cc_s[rows, :])).astype(bf16)
            delta = row_sum(ag.astype(f32) * af)
            out_ref[0, h] = ag
            lane = lanes_of((nb, 128))
            pack = jnp.zeros((nb, 128), f32)
            for i, x in enumerate(split3(low_half(rs_ref[h])) + split3(delta) + split3(st_s[rows, :])):
                pack = jnp.where(lane == i, x, pack)
            out_ref[1, h] = pack.astype(bf16)
            out_ref[2, h] = q1_ref[h]

    return rows_kernel


def grad_terms(attn, og, gain, rinv, cc):
    af = attn.astype(f32)
    gd = og.astype(f32) * gain
    ag = (rinv * (gd - af * cc)).astype(bf16).astype(f32)
    return af, ag, row_sum(ag * af)


def make_back_prev_kernel(feats):
    def back_prev_kernel(
        info, stat_ref, other_ref, q_ref, attn_ref, rr_ref, e_ref, og_ref, gain_ref, kv_ref,
        back_ref, dq_ref, rinv_s, cc_s,
    ):
        g = pl.program_id(0)
        h = 2 * g + info[2]
        tok = q_ref.shape[1]
        half = tok // 2
        scale = 1.0 / math.sqrt(q_ref.shape[2])

        @pl.when(g == 0)
        def _():
            rinv, cc = norm_terms(stat_ref, other_ref, feats)
            rinv_s[...] = spread(rinv)
            cc_s[...] = spread(cc)

        af, ag, delta = grad_terms(attn_ref[h], og_ref[0], gain_ref[0], rinv_s[...], cc_s[...])
        r = high_half(rr_ref[h])
        do = (ag * r).astype(bf16)
        dl = delta * r
        dk = jnp.zeros((128, tok), f32)
        dv = jnp.zeros((128, tok), f32)
        for c in range(2):
            sl = slice(c * half, (c + 1) * half)
            e = e_ref[g, sl, :]
            dp = dot_nt(do[sl], kv_ref[1, 0])
            ds = (e.astype(f32) * (dp - jnp.concatenate([dl[sl]] * (tok // 128), axis=1))).astype(bf16)
            dq_ref[g, sl, :] = dot_nn(ds, kv_ref[0, 0])
            dk = dk + dot_tn(q_ref[h, sl, :], ds)
            dv = dv + dot_tn(do[sl], e)
        back_ref[0, 0] = (dk * scale).T.astype(bf16)
        back_ref[1, 0] = dv.T.astype(bf16)

    return back_prev_kernel


def make_back_own_kernel(feats, first, aliased):
    def back_own_kernel(
        info, offs, stat_ref, other_ref, q_ref, k_ref, v_ref, attn_ref, rr_ref, e_ref, dqp_ref,
        og_ref, gain_ref, e1_ref, rs_ref, ga_ref, gb_ref, cos_ref, sin_ref, *refs
    ):
        normed_ref, gq_ref, dk_ref, dv_ref, rinv_s, cc_s, ag_s, de_s, dq_s = refs[aliased:]
        step = pl.program_id(0)
        h = step + first
        sel = info[2]
        tok = q_ref.shape[1]
        nb = e1_ref.shape[1]
        rate = tok // nb
        count = ga_ref.shape[2]
        half = tok // 2
        scale = 1.0 / math.sqrt(q_ref.shape[2])

        @pl.when(step == 0)
        def _():
            rinv, cc = norm_terms(stat_ref, other_ref, feats)
            rinv_s[...] = spread(rinv)
            cc_s[...] = spread(cc)

        rinv = rinv_s[...]
        af, ag, delta = grad_terms(attn_ref[h], og_ref[0], gain_ref[0], rinv, cc_s[...])
        normed_ref[0] = (af * rinv * gain_ref[0]).astype(bf16)
        ag_s[...] = ag
        de_s[...] = delta
        r = low_half(rr_ref[h])
        do = (ag * r).astype(bf16)
        dl = delta * r
        here = jnp.where(h % 2 == sel, 1.0, 0.0)
        dks = []
        for c in range(2):
            lo, n = c * half, (c + 1) * half
            sl = slice(lo, n)
            e = e_ref[h, sl, :n]
            dp = dot_nt(do[sl], v_ref[h, :n, :])
            ds = (e.astype(f32) * (dp - jnp.concatenate([dl[sl]] * (n // 128), axis=1))).astype(bf16)
            dq_s[sl, :] = dot_nn(ds, k_ref[h, :n, :]) + dqp_ref[h // 2, sl, :] * here
            dks.append((dot_tn(q_ref[h, sl, :], ds), dot_tn(do[sl], e)))
        for i, ref in enumerate((dk_ref, dv_ref)):
            ref[h, :half, :] = (dks[0][i] + dks[1][i][:, :half]).T
            ref[h, half:, :] = dks[1][i][:, half:].T

        rows = pl.ds(offs[h], nb, stride=rate)
        r1 = high_half(rs_ref[0])
        g1 = (ag_s[rows, :] * r1).astype(bf16)
        d1 = (de_s[rows, :] * r1)[:, :1]
        dq1 = jnp.zeros((nb, 128), f32)
        for part, ref in enumerate((ga_ref, gb_ref)):
            dp1 = dot_nt(g1, ref[1, 0])
            ds1 = (e1_ref[0, :, part * count : (part + 1) * count].astype(f32) * (dp1 - d1)).astype(bf16)
            dq1 = dq1 + dot_nn(ds1, ref[0, 0])
        dq_s[rows, :] += dq1
        cos, sin = unpack_tables(cos_ref, sin_ref)
        gq_ref[0] = rot(dq_s[...] * scale, cos, -sin).astype(bf16)

    return back_own_kernel


def make_final_kernel(codes):
    def final_kernel(
        info, offs, dk_ref, dv_ref, back_ref, rows_ref, sa_ref, sb_ref, cos_ref, sin_ref,
        gk_ref, gv_ref, dk_s, dv_s,
    ):
        g = pl.program_id(0)
        index, par = info[0], info[1]
        tok = dk_ref.shape[1]
        nb = rows_ref.shape[2]
        rate = tok // nb
        count = sa_ref.shape[2]
        scale = 1.0 / math.sqrt(dk_ref.shape[2])
        cos, sin = unpack_tables(cos_ref, sin_ref)
        kb = index * nb + rows_of((nb, count))
        pick = (rows_of((16, 128)) == lanes_of((16, 128))).astype(bf16)
        for hh in range(2):
            h = 2 * g + hh
            off = offs[h]
            here = (par == hh) & (index < info[3] - 1)
            dk_s[hh] = dk_ref[h] * scale + jnp.where(here, back_ref[0, 0].astype(f32), 0.0)
            dv_s[hh] = dv_ref[h] + jnp.where(here, back_ref[1, 0].astype(f32), 0.0)
            k1 = rows_ref[0, hh]
            v1 = rows_ref[1, hh]
            kpos = (off + rate * kb).astype(f32)
            dk1 = jnp.zeros((nb, 128), f32)
            dv1 = jnp.zeros((nb, 128), f32)
            for part, s in enumerate((sa_ref, sb_ref)):
                qb = key_order(index, codes, nb, part, count)
                st = dot_nt(pick, s[1, hh])
                lse = st[0:1] + st[1:2] + st[2:3]
                delta = st[3:4] + st[4:5] + st[5:6]
                start = st[6:7] + st[7:8] + st[8:9]
                ok = (kb <= qb) & (kpos >= start)
                z = jnp.where(ok, dot_nt(k1, s[2, hh]) * scale - lse, NEG)
                p = jnp.exp(z).astype(bf16)
                dp = dot_nt(v1, s[0, hh])
                ds = (p.astype(f32) * (dp - delta)).astype(bf16)
                dk1 = dk1 + dot_nn(ds, s[2, hh])
                dv1 = dv1 + dot_nn(p, s[0, hh])
            rows = pl.ds(off, nb, stride=rate)
            dk_s[hh, rows, :] += dk1 * scale
            dv_s[hh, rows, :] += dv1
            gk_ref[hh] = rot(dk_s[hh], cos, -sin).astype(bf16)
            gv_ref[hh] = dv_s[hh].astype(bf16)

    return final_kernel


def call(kernel, prefetch, grid, ins, outs, scratch=(), alias=(), cost=None):
    arrays, in_specs = [], []
    for a, b, m in ins:
        if b is None:
            arrays.append(pltpu.with_memory_space_constraint(a, pltpu.VMEM))
            in_specs.append(pl.BlockSpec(memory_space=pltpu.VMEM))
        else:
            arrays.append(a)
            in_specs.append(pl.BlockSpec(b, m))
    out_shape, out_specs = [], []
    for s, d, b, m in outs:
        if b is None:
            out_shape.append(pltpu.VMEM(s, d))
            out_specs.append(pl.BlockSpec(memory_space=pltpu.VMEM))
        else:
            out_shape.append(jax.ShapeDtypeStruct(s, d))
            out_specs.append(pl.BlockSpec(b, m))
    us = 4
    return pl.pallas_call(
        kernel,
        out_shape=out_shape,
        grid_spec=pltpu.PrefetchScalarGridSpec(
            num_scalar_prefetch=len(prefetch),
            grid=grid,
            in_specs=in_specs,
            out_specs=out_specs,
            scratch_shapes=list(scratch),
        ),
        input_output_aliases={len(prefetch) + i: o for i, o in alias},
        cost_estimate=pl.CostEstimate(flops=0, transcendentals=0, bytes_accessed=int(us * 3.0e6)),
        compiler_params=pltpu.CompilerParams(
            dimension_semantics=("arbitrary",) * len(grid), vmem_limit_bytes=24 << 20
        ),
    )(*prefetch, *arrays)


def after(x, *deps):
    return lax.optimization_barrier((x, *deps))[0]


def body(queries, keys, values, out_grad, norm_gain, doc_start, head_offsets):
    heads, tok, width = queries.shape
    ctx = lax.axis_size("ctx")
    rate = ctx * tok // SEL
    nb = tok // rate
    feats = float(HEADS * width)
    pairs = heads // 2
    index = lax.axis_index("ctx")
    base = index * tok
    codes = [1 << b for b in range(2, ctx.bit_length() - 1)] + [2, 1]

    starts = lax.dynamic_slice_in_dim(doc_start, base, tok)
    position = base + jnp.arange(tok, dtype=jnp.int32)
    rel = (position - starts).astype(f32)
    freq = theta_base ** (-2.0 * jnp.arange(width // 2).astype(f32) / width)
    angle = jnp.concatenate([rel[: tok // 2, None] * freq[None, :], rel[tok // 2 :, None] * freq[None, :]], axis=1)
    cos, sin = jnp.cos(angle), jnp.sin(angle)
    begin = starts.astype(f32).reshape(tok // 128, 128)
    start_rel = (starts - base).astype(f32).reshape(tok // 128, 128)
    info = jnp.stack([index, index % 2, (index + 1) % 2, jnp.int32(ctx)]).astype(jnp.int32)
    gain = norm_gain.reshape(heads, 1, width)

    pair3 = (2, tok, width)
    one3 = (1, tok, width)
    full = queries.shape
    const = lambda n: (lambda i, *s: (0,) * n)
    whole = lambda a: (a, a.shape, const(a.ndim))
    vm = lambda a: (a, None, None)
    gp = lambda g, *s: (g, 0, 0)
    g4 = lambda g, *s: (0, g, 0, 0)

    def swap(x, code):
        return lax.ppermute(x, "ctx", [(i, i ^ code) for i in range(ctx)])

    half_count = SEL // 2

    k_rot, vals, send, rows = call(
        prep_kernel, (info, head_offsets), (pairs,),
        [(keys, pair3, gp), (values, pair3, gp), whole(cos), whole(sin)],
        [
            (full, bf16, None, None),
            (full, bf16, None, None),
            ((2, pairs, tok, width), bf16, (2, 1, tok, width), g4),
            ((2, heads, nb, width), bf16, (2, 2, nb, width), g4),
        ],
    )
    lead, z_code, y_code, core = codes[:-3], codes[-3], codes[-2], codes[-1]
    recv = lax.ppermute(send, "ctx", [(i, i + 1) for i in range(ctx - 1)])

    def join2(x, code):
        return jnp.concatenate([x, swap(x, code)], axis=2)

    x = rows
    for code in lead:
        x = join2(x, code)

    def own(first, qs, prior):
        n = pairs // 2
        outs = [
            (full, bf16, None, None),
            ((heads, tok, tok), bf16, None, None),
            (full, f32, None, None),
            (full, f32, None, None),
            (full, f32, None, None),
            ((heads, nb, width), bf16, (2, nb, width), lambda g, *s: (g + first, 0, 0)),
        ]
        ins = [
            whole(start_rel),
            (qs, pair3, lambda g, *s: (g + first, 0, 0)),
            vm(k_rot), vm(vals), whole(cos), whole(sin),
        ]
        alias = []
        for i, a in enumerate(prior):
            alias.append((len(ins), i))
            ins.append(vm(a) if i < 5 else (a, (2, nb, width), lambda g, *s: (first, 0, 0)))
        return call(
            make_own_kernel(first, len(prior)), (info, head_offsets), (n,), ins, outs,
            [pltpu.VMEM((tok, tok), f32)], alias,
        )

    part = own(0, queries, [])
    x = after(x, part[3])
    y = join2(x, z_code)
    part = own(pairs // 2, after(queries, x), part)
    q_rot, e_own, acc, m_own, lsum, q1 = part
    y = after(y, m_own)
    ga = join2(y, y_code)

    acc, lsum, m_new, e_prev, m_prev = call(
        prev_kernel, (info,), (pairs,),
        [
            whole(start_rel), vm(after(q_rot, y)),
            (recv, (2, 1, tok, width), g4),
            vm(acc), vm(m_own), vm(lsum),
        ],
        [
            (full, f32, None, None),
            (full, f32, None, None),
            ((pairs, tok, width), f32, None, None),
            ((pairs, tok, tok), bf16, None, None),
            ((pairs, tok, width), f32, None, None),
        ],
        [pltpu.VMEM((tok, tok), f32)],
        [(3, 0), (5, 1)],
    )
    ga = after(ga, m_new)
    gb = swap(ga, core)

    attn, rr, e1, rs, attn_rows, og_rows, stat = call(
        make_join_kernel(codes), (info, head_offsets), (pairs,),
        [
            whole(start_rel), vm(acc), vm(m_own), vm(lsum), vm(m_new), vm(m_prev),
            (q1, (2, nb, width), gp),
            (ga, (2, 2, half_count, width), g4),
            (gb, (2, 2, half_count, width), g4),
            (out_grad, pair3, gp),
            (gain, (2, 1, width), gp),
        ],
        [
            (full, bf16, None, None),
            (full, f32, None, None),
            ((heads, nb, SEL), bf16, (2, nb, SEL), gp),
            ((heads, nb, width), f32, (2, nb, width), gp),
            ((heads, nb, width), bf16, (2, nb, width), gp),
            ((heads, nb, width), bf16, (2, nb, width), gp),
            ((2 * tok // 128, 128), f32, (2 * tok // 128, 128), const(2)),
        ],
        [pltpu.VMEM((tok, 128), f32)] + [pltpu.VMEM((2, tok, 128), f32)] * 3 + [pltpu.VMEM((tok, 128), f32)] * 2,
    )
    other = lax.ppermute(stat, "head", [(0, 1), (1, 0)])

    (x,) = call(
        make_rows_kernel(feats), (head_offsets,), (1,),
        [whole(begin), whole(stat), whole(other), whole(attn_rows), whole(og_rows), whole(q1), whole(gain), whole(rs)],
        [((3, heads, nb, width), bf16, (3, heads, nb, width), const(4))],
        [pltpu.VMEM((tok, 128), f32)] * 3,
    )
    rows1 = x
    for code in lead:
        x = join2(x, code)

    gsel = lambda g, s, *_: (2 * g + s[2], 0, 0)
    back, dq_prev = call(
        make_back_prev_kernel(feats), (info,), (pairs,),
        [
            whole(stat), whole(after(other, rows1)),
            vm(q_rot), vm(attn), vm(rr), vm(e_prev),
            (out_grad, one3, gsel),
            (gain, (1, 1, width), gsel),
            (recv, (2, 1, tok, width), g4),
        ],
        [
            ((2, pairs, tok, width), bf16, (2, 1, tok, width), g4),
            ((pairs, tok, width), f32, None, None),
        ],
        [pltpu.VMEM((tok, 128), f32)] * 2,
    )
    x = after(x, dq_prev)
    y = join2(x, z_code)
    back = lax.ppermute(back, "ctx", [(i + 1, i) for i in range(ctx - 1)])

    def back_own(first, dep, prior):
        n = heads // 2
        hp = lambda h, *s: (h + first, 0, 0)
        hg = lambda h, *s: (0, h + first, 0, 0)
        ins = [
            whole(stat), whole(after(other, dep)),
            vm(q_rot), vm(k_rot), vm(vals), vm(attn), vm(rr), vm(e_own), vm(dq_prev),
            (out_grad, one3, hp),
            (gain, (1, 1, width), hp),
            (e1, (1, nb, SEL), hp),
            (rs, (1, nb, width), hp),
            (ga, (2, 1, half_count, width), hg),
            (gb, (2, 1, half_count, width), hg),
            whole(cos), whole(sin),
        ]
        alias = []
        for i, a in enumerate(prior):
            alias.append((len(ins), i))
            ins.append(vm(a) if i >= 2 else (a, (1, 16, width), lambda h, *s: (first, 0, 0)))
        return call(
            make_back_own_kernel(feats, first, len(prior)), (info, head_offsets), (n,), ins,
            [
                (full, bf16, one3, hp),
                (full, bf16, one3, hp),
                (full, f32, None, None),
                (full, f32, None, None),
            ],
            [pltpu.VMEM((tok, 128), f32)] * 5,
            alias,
        )

    part = back_own(0, x, [])
    y = after(y, part[2])
    sa = join2(y, y_code)
    part = back_own(heads // 2, y, part)
    normed, grad_queries, dk_own, dv_own = part
    sa = after(sa, dk_own)
    sb = swap(sa, core)

    grad_keys, grad_values = call(
        make_final_kernel(codes), (info, head_offsets), (pairs,),
        [
            vm(dk_own), vm(dv_own),
            (back, (2, 1, tok, width), g4),
            (rows, (2, 2, nb, width), g4),
            (sa, (3, 2, half_count, width), g4),
            (sb, (3, 2, half_count, width), g4),
            whole(cos), whole(sin),
        ],
        [
            (full, bf16, pair3, gp),
            (full, bf16, pair3, gp),
        ],
        [pltpu.VMEM((2, tok, 128), f32)] * 2,
    )
    return (normed, grad_queries, grad_keys, grad_values)


def solution(mesh):
    return jax.shard_map(
        body,
        mesh=mesh,
        in_specs=(
            P("head", "ctx", None),
            P("head", "ctx", None),
            P("head", "ctx", None),
            P("head", "ctx", None),
            P("head", None),
            P(),
            P("head"),
        ),
        out_specs=(
            P("head", "ctx", None),
            P("head", "ctx", None),
            P("head", "ctx", None),
            P("head", "ctx", None),
        ),
        check_vma=False,
    )
```

```python
import math

import jax
import jax.numpy as jnp
from jax import lax
from jax.experimental import pallas as pl
from jax.experimental.pallas import tpu as pltpu
from jax.sharding import PartitionSpec as P

HEADS = 16
SEL = 256
theta_base = 10000.0
eps_norm = 1e-06
NEG = -1e30
f32 = jnp.float32
bf16 = jnp.bfloat16


def dot_nn(a, b):
    return lax.dot_general(a, b, (((1,), (0,)), ((), ())), preferred_element_type=f32)


def dot_nt(a, b):
    return lax.dot_general(a, b, (((1,), (1,)), ((), ())), preferred_element_type=f32)


def dot_tn(a, b):
    return lax.dot_general(a, b, (((0,), (0,)), ((), ())), preferred_element_type=f32)


def lanes_of(shape):
    return lax.broadcasted_iota(jnp.int32, shape, len(shape) - 1)


def rows_of(shape):
    return lax.broadcasted_iota(jnp.int32, shape, len(shape) - 2)


def low_half(x):
    return jnp.where(lanes_of(x.shape) < 64, x, pltpu.roll(x, 64, 1))


def high_half(x):
    return jnp.where(lanes_of(x.shape) < 64, pltpu.roll(x, 64, 1), x)


def unpack_tables(cos_ref, sin_ref):
    c, s = cos_ref[...], sin_ref[...]
    cos = jnp.concatenate([low_half(c), high_half(c)], axis=0)
    sin = jnp.concatenate([low_half(s), high_half(s)], axis=0)
    sin = jnp.where(lanes_of(sin.shape) < 64, -sin, sin)
    return cos, sin


def rot(x, cos, sin):
    return x * cos + pltpu.roll(x, 64, 1) * sin


def spread(row):
    parts = []
    for i in range(row.shape[0]):
        parts.append(jnp.broadcast_to(row[i : i + 1, :], (128, 128)).T)
    return jnp.concatenate(parts, axis=0)


def compact(x):
    eye = rows_of((128, 128)) == lanes_of((128, 128))
    parts = []
    for i in range(x.shape[0] // 128):
        block = x[i * 128 : (i + 1) * 128, :]
        parts.append(jnp.sum(jnp.where(eye, block, 0.0), axis=0, keepdims=True))
    return jnp.concatenate(parts, axis=0)


def row_sum(x):
    return jnp.broadcast_to(jnp.sum(x, axis=1, keepdims=True), x.shape)


def prep_kernel(info, k_ref, v_ref, cos_ref, sin_ref, kr_ref, rows_ref):
    g = pl.program_id(0)
    tok = k_ref.shape[1]
    nb = rows_ref.shape[2]
    rate = tok // nb
    cos, sin = unpack_tables(cos_ref, sin_ref)
    for hh in range(2):
        h = 2 * g + hh
        hot = (lanes_of((nb, tok)) == info[4 + h] + rate * rows_of((nb, tok))).astype(bf16)
        kr = rot(k_ref[h].astype(f32), cos, sin).astype(bf16)
        kr_ref[h] = kr
        rows_ref[0, hh] = dot_nn(hot, kr).astype(bf16)
        rows_ref[1, hh] = dot_nn(hot, v_ref[h]).astype(bf16)


def make_own_kernel(first, aliased):
    def own_kernel(info, start_ref, q_ref, k_ref, v_ref, cos_ref, sin_ref, *refs):
        refs = refs[aliased:]
        qr_ref, e_ref, acc_ref, m_ref, l_ref, rows_ref, bias_ref = refs
        tok = q_ref.shape[1]
        nb = rows_ref.shape[1]
        rate = tok // nb
        half = tok // 2
        scale = 1.0 / math.sqrt(q_ref.shape[2])

        @pl.when(pl.program_id(0) == 0)
        def _():
            start = spread(start_ref[...])
            for c in range(tok // 128):
                key = lanes_of((tok, 128)) + c * 128
                ok = (key <= rows_of((tok, 128))) & (key.astype(f32) >= start)
                bias_ref[:, c * 128 : (c + 1) * 128] = jnp.where(ok, 0.0, NEG)

        cos, sin = unpack_tables(cos_ref, sin_ref)
        for hh in range(2):
            h = 2 * (pl.program_id(0) + first) + hh
            q = rot(q_ref[hh].astype(f32), cos, sin).astype(bf16)
            qr_ref[h] = q
            hot = (lanes_of((nb, tok)) == info[4 + h] + rate * rows_of((nb, tok))).astype(bf16)
            rows_ref[hh] = dot_nn(hot, q).astype(bf16)
            vals = jnp.concatenate([v_ref[h], jnp.ones((tok, 128), bf16)], axis=1)
            for c in range(2):
                lo, n = c * half, (c + 1) * half
                z = dot_nt(q[lo:n], k_ref[h, :n, :]) * scale + bias_ref[lo:n, :n]
                m = jnp.max(z, axis=1, keepdims=True)
                e = jnp.exp(z - m).astype(bf16)
                e_ref[h, lo:n, :n] = e
                out = dot_nn(e, vals[:n])
                acc_ref[h, lo:n, :] = out[:, :128]
                l_ref[h, lo:n, :] = out[:, 128:]
                m_ref[h, lo:n, :] = jnp.broadcast_to(m, (half, 128))

    return own_kernel


def split3(x):
    hi = x.astype(bf16).astype(f32)
    mid = (x - hi).astype(bf16).astype(f32)
    return hi, mid, x - hi - mid


def pack3(parts, rows):
    stack = [p for x in parts for p in split3(x)]
    used = sum(p.shape[0] for p in stack)
    if used < rows:
        stack.append(jnp.zeros((rows - used, 128), f32))
    return jnp.concatenate(stack, axis=0).astype(bf16)


def unpack3(block, n, which):
    x = block.astype(f32)
    i = 3 * n * which
    return x[i : i + n] + x[i + n : i + 2 * n] + x[i + 2 * n : i + 3 * n]


def next_kernel(info, start_ref, q_ref, k_ref, v_ref, cos_ref, sin_ref, o_ref, e_ref, qn_ref, bias_ref, m_s, l_s):
    g = pl.program_id(0)
    tok = q_ref.shape[1]
    half = tok // 2
    scale = 1.0 / math.sqrt(q_ref.shape[2])
    h = 2 * g + info[1]

    @pl.when(g == 0)
    def _():
        start = spread(start_ref[...])
        for c in range(tok // 128):
            key = (lanes_of((tok, 128)) + c * 128).astype(f32)
            bias_ref[:, c * 128 : (c + 1) * 128] = jnp.where(key >= start, 0.0, NEG)

    cos, sin = unpack_tables(cos_ref, sin_ref)
    q = rot(q_ref[0].astype(f32), cos, sin).astype(bf16)
    qn_ref[g] = q
    vals = jnp.concatenate([v_ref[h], jnp.ones((tok, 128), bf16)], axis=1)
    for c in range(2):
        sl = slice(c * half, (c + 1) * half)
        z = dot_nt(q[sl], k_ref[h]) * scale + bias_ref[sl, :]
        m = jnp.max(z, axis=1, keepdims=True)
        e = jnp.exp(z - m).astype(bf16)
        e_ref[g, sl, :] = e
        out = dot_nn(e, vals)
        o_ref[0, sl, :] = out[:, :128].astype(bf16)
        m_s[sl, :] = jnp.broadcast_to(m, (half, 128))
        l_s[sl, :] = out[:, 128:]
    o_ref[0, tok:, :] = pack3((compact(m_s[...]), compact(l_s[...])), o_ref.shape[1] - tok)


def key_order(index, codes, nb, part, count):
    col = lanes_of((1, count)) + part * count
    slot = col // nb
    dev = jnp.full((1, count), index, jnp.int32)
    for b, code in enumerate(codes):
        dev = dev ^ (((slot >> b) & 1) * code)
    return dev * nb + col % nb


def make_join_kernel(codes):
    def join_kernel(
        info, start_ref, acc_ref, m_ref, l_ref, on_ref, q1_ref, ga_ref, gb_ref, og_ref, gain_ref,
        attn_ref, rr_ref, e1_ref, rs_ref, ar_ref, or_ref, stat_ref,
        start_s, m_s, l_s, acc_s, sq_s, cr_s,
    ):
        g = pl.program_id(0)
        index, sel = info[0], info[2]
        tok = og_ref.shape[1]
        nb = q1_ref.shape[1]
        rate = tok // nb
        count = ga_ref.shape[2]
        scale = 1.0 / math.sqrt(og_ref.shape[2])

        @pl.when(g == 0)
        def _():
            start_s[...] = spread(start_ref[...])
            sq_s[...] = jnp.zeros_like(sq_s)
            cr_s[...] = jnp.zeros_like(cr_s)

        stats = on_ref[0, tok:, :]
        n = tok // 128
        ok = index > 0
        m_prev = jnp.where(ok, spread(unpack3(stats, n, 0)), NEG)
        l_prev = spread(unpack3(stats, n, 1))
        m_own = m_ref[2 * g + sel]
        mn = jnp.maximum(m_own, m_prev)
        a_own = jnp.exp(m_own - mn)
        a_prev = jnp.where(ok, jnp.exp(m_prev - mn), 0.0)
        m_s[sel] = mn
        l_s[sel] = a_own * l_ref[2 * g + sel] + a_prev * l_prev
        acc_s[sel] = a_own * acc_ref[2 * g + sel] + a_prev * on_ref[0, :tok, :].astype(f32)
        m_s[1 - sel] = m_ref[2 * g + 1 - sel]
        l_s[1 - sel] = l_ref[2 * g + 1 - sel]
        acc_s[1 - sel] = acc_ref[2 * g + 1 - sel]

        for hh in range(2):
            h = 2 * g + hh
            off = info[4 + h]
            rows = pl.ds(off, nb, stride=rate)
            here = sel == hh
            m_own = m_ref[h]

            q1 = q1_ref[hh]
            start1 = start_s[rows, :][:, :1]
            qb = index * nb + rows_of((nb, count))
            zs = []
            for part, ref in enumerate((ga_ref, gb_ref)):
                kb = key_order(index, codes, nb, part, count)
                pos = (off + rate * kb - index * tok).astype(f32)
                ok = (kb <= qb) & (pos >= start1)
                zs.append(jnp.where(ok, dot_nt(q1, ref[0, hh]) * scale, NEG))
            m1 = jnp.maximum(jnp.max(zs[0], axis=1, keepdims=True), jnp.max(zs[1], axis=1, keepdims=True))
            o1 = jnp.zeros((nb, 256), f32)
            for part, ref in enumerate((ga_ref, gb_ref)):
                e1 = jnp.exp(zs[part] - m1).astype(bf16)
                e1_ref[hh, :, part * count : (part + 1) * count] = e1
                v1 = jnp.concatenate([ref[1, hh], jnp.ones((count, 128), bf16)], axis=1)
                o1 = o1 + dot_nn(e1, v1)

            mr = m_s[hh, rows, :]
            lr = l_s[hh, rows, :]
            ar = acc_s[hh, rows, :]
            m1b = jnp.broadcast_to(m1, (nb, 128))
            mn = jnp.maximum(mr, m1b)
            b0 = jnp.exp(mr - mn)
            b1 = jnp.exp(m1b - mn)
            ln = b0 * lr + b1 * o1[:, 128:]
            m_s[hh, rows, :] = mn
            l_s[hh, rows, :] = ln
            acc_s[hh, rows, :] = b0 * ar + b1 * o1[:, :128]
            lse1 = mn + jnp.log(ln)
            rs_ref[hh] = jnp.where(lanes_of((nb, 128)) < 64, lse1, b1 / ln)

            inv = 1.0 / l_s[hh]
            attn = (acc_s[hh] * inv).astype(bf16)
            attn_ref[h] = attn
            both = jnp.where((lanes_of((tok, 128)) < 64) | jnp.logical_not(here), m_own, m_prev)
            rr_ref[h] = jnp.exp(both - m_s[hh]) * inv
            af = attn.astype(f32)
            gd = og_ref[hh].astype(f32) * gain_ref[hh]
            sq_s[...] += af * af
            cr_s[...] += gd * af
            hot = (lanes_of((nb, tok)) == off + rate * rows_of((nb, tok))).astype(bf16)
            ar_ref[hh] = dot_nn(hot, attn).astype(bf16)
            or_ref[hh] = dot_nn(hot, og_ref[hh]).astype(bf16)

        @pl.when(g == pl.num_programs(0) - 1)
        def _():
            stat_ref[...] = jnp.concatenate([compact(row_sum(sq_s[...])), compact(row_sum(cr_s[...]))], axis=0)

    return join_kernel


def norm_terms(stat_ref, other_ref, feats):
    total = stat_ref[...] + other_ref[...]
    n = total.shape[0] // 2
    rinv = lax.rsqrt(total[:n] / feats + eps_norm)
    return rinv, rinv * rinv * total[n:] / feats


def split3(x):
    hi = x.astype(bf16).astype(f32)
    mid = (x - hi).astype(bf16).astype(f32)
    return hi, mid, x - hi - mid


def grad_terms(attn, og, gain, rinv, cc):
    af = attn.astype(f32)
    gd = og.astype(f32) * gain
    ag = (rinv * (gd - af * cc)).astype(bf16).astype(f32)
    return af, ag, row_sum(ag * af)


def make_rows_kernel(feats):
    def rows_kernel(
        info, begin_ref, stat_ref, other_ref, ar_ref, or_ref, q1_ref, gain_ref, rs_ref, attn_ref, rr_ref, og_ref,
        out_ref, st_ref, do_ref, rinv_s, cc_s, st_s,
    ):
        g = pl.program_id(0)
        sel = info[2]
        nb = ar_ref.shape[1]
        tok = og_ref.shape[1]
        rate = tok // nb

        @pl.when(g == 0)
        def _():
            rinv, cc = norm_terms(stat_ref, other_ref, feats)
            rinv_s[...] = spread(rinv)
            cc_s[...] = spread(cc)
            st_s[...] = spread(begin_ref[...])
            st_ref[...] = jnp.zeros_like(st_ref)

        for hh in range(2):
            rows = pl.ds(info[4 + 2 * g + hh], nb, stride=rate)
            af = ar_ref[hh].astype(f32)
            gd = or_ref[hh].astype(f32) * gain_ref[hh]
            ag = (rinv_s[rows, :] * (gd - af * cc_s[rows, :])).astype(bf16)
            delta = row_sum(ag.astype(f32) * af)
            out_ref[0, hh] = ag
            lane = lanes_of((nb, 128))
            spot = lane == (2 * g + hh) * nb + rows_of((nb, 128))
            for i, x in enumerate(split3(low_half(rs_ref[hh])) + split3(delta) + split3(st_s[rows, :])):
                st_ref[i : i + 1, :] += jnp.sum(jnp.where(spot, x, 0.0), axis=0, keepdims=True)
            out_ref[1, hh] = q1_ref[hh]

        h = 2 * g + sel
        af, ag, delta = grad_terms(attn_ref[h], og_ref[0], gain_ref[sel], rinv_s[...], cc_s[...])
        r = high_half(rr_ref[h])
        do_ref[0, :tok, :] = (ag * r).astype(bf16)
        do_ref[0, tok:, :] = pack3((compact(delta * r),), do_ref.shape[1] - tok)

    return rows_kernel


def next_back_kernel(info, do_ref, q_ref, k_ref, v_ref, e_ref, dq_ref, dk_ref, dv_ref):
    g = pl.program_id(0)
    h = 2 * g + info[1]
    tok = q_ref.shape[1]
    half = tok // 2
    scale = 1.0 / math.sqrt(q_ref.shape[2])
    dl = spread(unpack3(do_ref[0, tok:, :], tok // 128, 0))
    dk = jnp.zeros((128, tok), f32)
    dv = jnp.zeros((128, tok), f32)
    for c in range(2):
        sl = slice(c * half, (c + 1) * half)
        e = e_ref[g, sl, :]
        do = do_ref[0, sl, :]
        dp = dot_nt(do, v_ref[h])
        ds = (e.astype(f32) * (dp - jnp.concatenate([dl[sl]] * (tok // 128), axis=1))).astype(bf16)
        dq_ref[0, sl, :] = (dot_nn(ds, k_ref[h]) * scale).astype(bf16)
        dk = dk + dot_tn(q_ref[g, sl, :], ds)
        dv = dv + dot_tn(do, e)
    dk_ref[g] = dk.T
    dv_ref[g] = dv.T


def make_back_own_kernel(feats, first, aliased):
    def back_own_kernel(
        info, stat_ref, other_ref, q_ref, k_ref, v_ref, attn_ref, rr_ref, e_ref,
        og_ref, gain_ref, e1_ref, rs_ref, ga_ref, gb_ref, *refs
    ):
        normed_ref, dq_ref, dk_ref, dv_ref, rinv_s, cc_s, ag_s, de_s = refs[aliased:]
        step = pl.program_id(0)
        h = step + first
        tok = q_ref.shape[1]
        nb = e1_ref.shape[1]
        rate = tok // nb
        count = ga_ref.shape[2]
        half = tok // 2

        @pl.when(step == 0)
        def _():
            rinv, cc = norm_terms(stat_ref, other_ref, feats)
            rinv_s[...] = spread(rinv)
            cc_s[...] = spread(cc)

        rinv = rinv_s[...]
        af, ag, delta = grad_terms(attn_ref[h], og_ref[0], gain_ref[0], rinv, cc_s[...])
        normed_ref[0] = (af * rinv * gain_ref[0]).astype(bf16)
        ag_s[...] = ag
        de_s[...] = delta
        r = low_half(rr_ref[h])
        do = (ag * r).astype(bf16)
        dl = delta * r
        dks = []
        for c in range(2):
            lo, n = c * half, (c + 1) * half
            sl = slice(lo, n)
            e = e_ref[h, sl, :n]
            dp = dot_nt(do[sl], v_ref[h, :n, :])
            ds = (e.astype(f32) * (dp - jnp.concatenate([dl[sl]] * (n // 128), axis=1))).astype(bf16)
            dq_ref[h, sl, :] = dot_nn(ds, k_ref[h, :n, :])
            dks.append((dot_tn(q_ref[h, sl, :], ds), dot_tn(do[sl], e)))
        for i, ref in enumerate((dk_ref, dv_ref)):
            ref[h, :half, :] = (dks[0][i] + dks[1][i][:, :half]).T
            ref[h, half:, :] = dks[1][i][:, half:].T

        rows = pl.ds(info[4 + h], nb, stride=rate)
        r1 = high_half(rs_ref[0])
        g1 = (ag_s[rows, :] * r1).astype(bf16)
        d1 = (de_s[rows, :] * r1)[:, :1]
        dq1 = jnp.zeros((nb, 128), f32)
        for part, ref in enumerate((ga_ref, gb_ref)):
            dp1 = dot_nt(g1, ref[1, 0])
            ds1 = (e1_ref[0, :, part * count : (part + 1) * count].astype(f32) * (dp1 - d1)).astype(bf16)
            dq1 = dq1 + dot_nn(ds1, ref[0, 0])
        dq_ref[h, rows, :] += dq1

    return back_own_kernel


def make_final_kernel(codes):
    def final_kernel(
        info, dq_ref, dk_ref, dv_ref, dkn_ref, dvn_ref, dqn_ref, rows_ref, sa_ref, sb_ref, ta_ref, tb_ref, cos_ref, sin_ref,
        gq_ref, gk_ref, gv_ref, dk_s, dv_s,
    ):
        g = pl.program_id(0)
        index, par, sel = info[0], info[1], info[2]
        tok = dk_ref.shape[1]
        nb = rows_ref.shape[2]
        rate = tok // nb
        count = sa_ref.shape[2]
        scale = 1.0 / math.sqrt(dk_ref.shape[2])
        cos, sin = unpack_tables(cos_ref, sin_ref)
        kb = index * nb + rows_of((nb, count))
        slots = ta_ref.shape[0]
        keep = rows_of((slots * 16, count)) // 16 == lanes_of((slots * 16, count)) // nb
        fold = (rows_of((16, slots * 16)) == lanes_of((16, slots * 16)) % 16).astype(bf16)
        for hh in range(2):
            h = 2 * g + hh
            off = info[4 + h]
            dq = dq_ref[h] * scale + jnp.where(sel == hh, dqn_ref[0].astype(f32), 0.0)
            gq_ref[hh] = rot(dq, cos, -sin).astype(bf16)
            here = par == hh
            dk_s[hh] = (dk_ref[h] + jnp.where(here, dkn_ref[g], 0.0)) * scale
            dv_s[hh] = dv_ref[h] + jnp.where(here, dvn_ref[g], 0.0)
            k1 = rows_ref[0, hh]
            v1 = rows_ref[1, hh]
            kpos = (off + rate * kb).astype(f32)
            dk1 = jnp.zeros((nb, 128), f32)
            dv1 = jnp.zeros((nb, 128), f32)
            pick = (rows_of((128, count)) == h * nb + lanes_of((128, count)) % nb).astype(bf16)
            for part, (s, t) in enumerate(((sa_ref, ta_ref), (sb_ref, tb_ref))):
                qb = key_order(index, codes, nb, part, count)
                each = dot_nn(t[...].reshape(slots * 16, 128), pick)
                st = dot_nn(fold, jnp.where(keep, each, 0.0).astype(bf16))
                lse = st[0:1] + st[1:2] + st[2:3]
                delta = st[3:4] + st[4:5] + st[5:6]
                start = st[6:7] + st[7:8] + st[8:9]
                ok = (kb <= qb) & (kpos >= start)
                z = jnp.where(ok, dot_nt(k1, s[1, hh]) * scale - lse, NEG)
                p = jnp.exp(z).astype(bf16)
                dp = dot_nt(v1, s[0, hh])
                ds = (p.astype(f32) * (dp - delta)).astype(bf16)
                dk1 = dk1 + dot_nn(ds, s[1, hh])
                dv1 = dv1 + dot_nn(p, s[0, hh])
            rows = pl.ds(off, nb, stride=rate)
            dk_s[hh, rows, :] += dk1 * scale
            dv_s[hh, rows, :] += dv1
            gk_ref[hh] = rot(dk_s[hh], cos, -sin).astype(bf16)
            gv_ref[hh] = dv_s[hh].astype(bf16)

    return final_kernel


def call(kernel, prefetch, grid, ins, outs, scratch=(), alias=(), cost=None):
    arrays, in_specs = [], []
    for a, b, m in ins:
        if b is None:
            arrays.append(pltpu.with_memory_space_constraint(a, pltpu.VMEM))
            in_specs.append(pl.BlockSpec(memory_space=pltpu.VMEM))
        else:
            arrays.append(a)
            in_specs.append(pl.BlockSpec(b, m))
    out_shape, out_specs = [], []
    for s, d, b, m in outs:
        if b is None:
            out_shape.append(pltpu.VMEM(s, d))
            out_specs.append(pl.BlockSpec(memory_space=pltpu.VMEM))
        else:
            out_shape.append(jax.ShapeDtypeStruct(s, d))
            out_specs.append(pl.BlockSpec(b, m))
    us = 4
    return pl.pallas_call(
        kernel,
        out_shape=out_shape,
        grid_spec=pltpu.PrefetchScalarGridSpec(
            num_scalar_prefetch=len(prefetch),
            grid=grid,
            in_specs=in_specs,
            out_specs=out_specs,
            scratch_shapes=list(scratch),
        ),
        input_output_aliases={len(prefetch) + i: o for i, o in alias},
        cost_estimate=pl.CostEstimate(flops=0, transcendentals=0, bytes_accessed=int(us * 3.0e6)),
        compiler_params=pltpu.CompilerParams(
            dimension_semantics=("arbitrary",) * len(grid), vmem_limit_bytes=24 << 20
        ),
    )(*prefetch, *arrays)


def after(x, *deps):
    return lax.optimization_barrier((x, *deps))[0]


def body(queries, keys, values, out_grad, norm_gain, doc_start, head_offsets):
    heads, tok, width = queries.shape
    ctx = lax.axis_size("ctx")
    rate = ctx * tok // SEL
    nb = tok // rate
    feats = float(HEADS * width)
    pairs = heads // 2
    index = lax.axis_index("ctx")
    base = index * tok
    codes = [1 << b for b in range(2, ctx.bit_length() - 1)] + [2, 1]

    starts = lax.dynamic_slice_in_dim(doc_start, base, tok)
    position = base + jnp.arange(tok, dtype=jnp.int32)
    rel = (position - starts).astype(f32)
    freq = theta_base ** (-2.0 * jnp.arange(width // 2).astype(f32) / width)

    def tables(rel):
        angle = jnp.concatenate([rel[: tok // 2, None] * freq, rel[tok // 2 :, None] * freq], axis=1)
        return jnp.cos(angle), jnp.sin(angle)

    cos, sin = tables(rel)
    begin = starts.astype(f32).reshape(tok // 128, 128)
    after_starts = lax.dynamic_slice_in_dim(doc_start, jnp.minimum(base + tok, (ctx - 1) * tok), tok)
    next_start = (after_starts - base).astype(f32).reshape(tok // 128, 128)
    rel_next = (position + tok - after_starts).astype(f32)
    cos_next, sin_next = tables(rel_next)
    start_rel = (starts - base).astype(f32).reshape(tok // 128, 128)
    spot = jnp.arange(4 + heads, dtype=jnp.int32)
    info = jnp.pad(head_offsets, (4, 0)).astype(jnp.int32)
    info = info + jnp.where(spot == 0, index, 0) + jnp.where(spot == 1, index % 2, 0) + jnp.where(spot == 2, (index + 1) % 2, 0)
    gain = norm_gain.reshape(heads, 1, width)

    pair3 = (2, tok, width)
    one3 = (1, tok, width)
    full = queries.shape
    const = lambda n: (lambda i, *s: (0,) * n)
    whole = lambda a: (a, a.shape, const(a.ndim))
    vm = lambda a: (a, None, None)
    hbm = lambda a: pltpu.with_memory_space_constraint(a, pltpu.HBM)
    gp = lambda g, *s: (g, 0, 0)
    g4 = lambda g, *s: (0, g, 0, 0)

    def swap(x, code):
        return lax.ppermute(x, "ctx", [(i, i ^ code) for i in range(ctx)])

    half_count = SEL // 2

    up = [(i, i + 1) for i in range(ctx - 1)]
    down = [(i + 1, i) for i in range(ctx - 1)]
    mine = lambda g, s, *_: (2 * g + s[2], 0, 0)
    lead, z_code, y_code, core = codes[:-3], codes[-3], codes[-2], codes[-1]

    def join2(x, code, *deps):
        y = swap(x, code)
        return jnp.concatenate([x, after(y, *deps) if deps else y], axis=2)

    q_send = lax.dynamic_index_in_dim(queries.reshape(pairs, 2, tok, width), (index + 1) % 2, 1, keepdims=False)
    q_raw = lax.ppermute(q_send, "ctx", down)
    k_rot, rows = call(
        prep_kernel, (info,), (pairs,),
        [vm(keys), vm(values), whole(cos), whole(sin)],
        [
            (full, bf16, None, None),
            ((2, heads, nb, width), bf16, (2, 2, nb, width), g4),
        ],
    )
    vals = values
    x = rows
    for code in lead[:-1]:
        x = join2(x, code)
    ahead = [swap(x, code) for code in lead[-1:]]

    def own(first, n, qs, prior):
        outs = [
            (full, bf16, None, None),
            ((heads, tok, tok), bf16, None, None),
            (full, f32, None, None),
            (full, f32, None, None),
            (full, f32, None, None),
            ((heads, nb, width), bf16, (2, nb, width), lambda g, *s: (g + first, 0, 0)),
        ]
        ins = [
            whole(start_rel),
            (qs, pair3, lambda g, *s: (g + first, 0, 0)),
            vm(k_rot), vm(vals), whole(cos), whole(sin),
        ]
        alias = []
        for i, a in enumerate(prior):
            alias.append((len(ins), i))
            ins.append(vm(a) if i < 5 else (a, (2, nb, width), lambda g, *s: (first, 0, 0)))
        return call(
            make_own_kernel(first, len(prior)), (info,), (n,), ins, outs,
            [pltpu.VMEM((tok, tok), f32)], alias,
        )

    part = own(0, pairs // 2, queries, [])
    for a in ahead:
        x = jnp.concatenate([x, after(a, part[3])], axis=2)
    x = after(x, part[3])
    pending = swap(x, z_code)
    extra = -(-6 * (tok // 128) // 16) * 16
    o_send, e_next, q_next = call(
        next_kernel, (info,), (pairs,),
        [
            whole(next_start),
            (after(q_raw, x), one3, gp),
            vm(k_rot), vm(vals), whole(cos_next), whole(sin_next),
        ],
        [
            ((pairs, tok + extra, width), bf16, (1, tok + extra, width), gp),
            ((pairs, tok, tok), bf16, None, None),
            ((pairs, tok, width), bf16, None, None),
        ],
        [pltpu.VMEM((tok, tok), f32)] + [pltpu.VMEM((tok, 128), f32)] * 2,
    )
    y = jnp.concatenate([x, after(pending, e_next)], axis=2)
    pending = swap(y, y_code)
    o_prev = lax.ppermute(o_send, "ctx", up)
    q_rot, e_own, acc, m_own, lsum, q1 = own(pairs // 2, pairs - pairs // 2, after(queries, y), part)
    ga = jnp.concatenate([y, after(pending, m_own)], axis=2)
    gb = swap(ga, core)

    attn, rr, e1, rs, attn_rows, og_rows, stat = call(
        make_join_kernel(codes), (info,), (pairs,),
        [
            whole(start_rel), vm(acc), vm(m_own), vm(lsum),
            (o_prev, (1, tok + extra, width), gp),
            (q1, (2, nb, width), gp),
            (ga, (2, 2, half_count, width), g4),
            (gb, (2, 2, half_count, width), g4),
            (out_grad, pair3, gp),
            (gain, (2, 1, width), gp),
        ],
        [
            (full, bf16, None, None),
            (full, f32, None, None),
            ((heads, nb, SEL), bf16, (2, nb, SEL), gp),
            ((heads, nb, width), f32, (2, nb, width), gp),
            ((heads, nb, width), bf16, (2, nb, width), gp),
            ((heads, nb, width), bf16, (2, nb, width), gp),
            ((2 * tok // 128, 128), f32, (2 * tok // 128, 128), const(2)),
        ],
        [pltpu.VMEM((tok, 128), f32)] + [pltpu.VMEM((2, tok, 128), f32)] * 3 + [pltpu.VMEM((tok, 128), f32)] * 2,
    )
    other = lax.ppermute(stat, "head", [(0, 1), (1, 0)])

    more = -(-3 * (tok // 128) // 16) * 16
    rows1, stats1, do_send = call(
        make_rows_kernel(feats), (info,), (pairs,),
        [
            whole(begin), whole(stat), whole(other),
            (attn_rows, (2, nb, width), gp),
            (og_rows, (2, nb, width), gp),
            (q1, (2, nb, width), gp),
            (gain, (2, 1, width), gp),
            (rs, (2, nb, width), gp),
            vm(attn), vm(rr),
            (out_grad, one3, mine),
        ],
        [
            ((2, heads, nb, width), bf16, (2, 2, nb, width), g4),
            ((16, 128), f32, (16, 128), const(2)),
            ((pairs, tok + more, width), bf16, (1, tok + more, width), gp),
        ],
        [pltpu.VMEM((tok, 128), f32)] * 3,
    )
    flat = jnp.concatenate([rows1.reshape(2 * heads * nb, width), stats1.astype(bf16)], axis=0)[None]

    def join0(x, y):
        return jnp.concatenate([x, y], axis=0)

    x = flat
    for code in lead[:-1]:
        x = join0(x, swap(x, code))
    ahead = [swap(x, code) for code in lead[-1:]]
    do_next = lax.ppermute(do_send, "ctx", down)

    def back_own(first, n, deps, prior):
        hp = lambda h, *s: (h + first, 0, 0)
        hg = lambda h, *s: (0, h + first, 0, 0)
        ins = [
            whole(stat), whole(after(other, *deps)),
            vm(q_rot), vm(k_rot), vm(vals), vm(attn), vm(rr), vm(e_own),
            (out_grad, one3, hp),
            (gain, (1, 1, width), hp),
            (e1, (1, nb, SEL), hp),
            (rs, (1, nb, width), hp),
            (ga, (2, 1, half_count, width), hg),
            (gb, (2, 1, half_count, width), hg),
        ]
        alias = []
        for i, a in enumerate(prior):
            alias.append((len(ins), i))
            ins.append(vm(a) if i >= 1 else (a, (1, 16, width), lambda h, *s: (first, 0, 0)))
        return call(
            make_back_own_kernel(feats, first, len(prior)), (info,), (n,), ins,
            [
                (full, bf16, one3, hp),
                (full, f32, None, None),
                (full, f32, None, None),
                (full, f32, None, None),
            ],
            [pltpu.VMEM((tok, 128), f32)] * 4,
            alias,
        )

    cut = heads // 2 + 1
    part = back_own(0, cut, (flat,), [])
    for a in ahead:
        x = join0(x, after(a, part[2]))
    x = after(x, part[2])
    pending = swap(x, z_code)

    dq_send, dk_next, dv_next = call(
        next_back_kernel, (info,), (pairs,),
        [
            (after(do_next, x), (1, tok + more, width), gp),
            vm(q_next), vm(k_rot), vm(vals), vm(e_next),
        ],
        [
            ((pairs, tok, width), bf16, one3, gp),
            ((pairs, tok, width), f32, None, None),
            ((pairs, tok, width), f32, None, None),
        ],
    )
    y = join0(x, after(pending, dk_next))
    pending = swap(y, y_code)
    dq_prev = lax.ppermute(dq_send, "ctx", up)
    normed, dq_own, dk_own, dv_own = back_own(cut, heads - cut, (y,), part)
    sa = after(join0(y, after(pending, dk_own)), dq_prev)
    sb = swap(sa, core)

    def sort(x):
        slots = x.shape[0]
        near = x[:, : 2 * heads * nb].reshape(slots, 2, heads, nb, width)
        near = near.transpose(1, 2, 0, 3, 4).reshape(2, heads, slots * nb, width)
        return near, x[:, 2 * heads * nb :]

    (sa, ta), (sb, tb) = sort(sa), sort(sb)
    grad_queries, grad_keys, grad_values = call(
        make_final_kernel(codes), (info,), (pairs,),
        [
            vm(dq_own), vm(dk_own), vm(dv_own), vm(dk_next), vm(dv_next),
            (dq_prev, one3, gp),
            (rows, (2, 2, nb, width), g4),
            (sa, (2, 2, half_count, width), g4),
            (sb, (2, 2, half_count, width), g4),
            whole(ta), whole(tb),
            whole(cos), whole(sin),
        ],
        [
            (full, bf16, pair3, gp),
            (full, bf16, pair3, gp),
            (full, bf16, pair3, gp),
        ],
        [pltpu.VMEM((2, tok, 128), f32)] * 2,
    )
    return (normed, grad_queries, grad_keys, grad_values)


def solution(mesh):
    return jax.shard_map(
        body,
        mesh=mesh,
        in_specs=(
            P("head", "ctx", None),
            P("head", "ctx", None),
            P("head", "ctx", None),
            P("head", "ctx", None),
            P("head", None),
            P(),
            P("head"),
        ),
        out_specs=(
            P("head", "ctx", None),
            P("head", "ctx", None),
            P("head", "ctx", None),
            P("head", "ctx", None),
        ),
        check_vma=False,
    )
```

```python
import math

import jax
import jax.numpy as jnp
from jax import lax
from jax.experimental import pallas as pl
from jax.experimental.pallas import tpu as pltpu
from jax.sharding import PartitionSpec as P

HEADS = 16
SEL = 256
theta_base = 10000.0
eps_norm = 1e-06
NEG = -1e30
f32 = jnp.float32
bf16 = jnp.bfloat16


def dot_nn(a, b):
    return lax.dot_general(a, b, (((1,), (0,)), ((), ())), preferred_element_type=f32)


def dot_nt(a, b):
    return lax.dot_general(a, b, (((1,), (1,)), ((), ())), preferred_element_type=f32)


def dot_tn(a, b):
    return lax.dot_general(a, b, (((0,), (0,)), ((), ())), preferred_element_type=f32)


def lanes_of(shape):
    return lax.broadcasted_iota(jnp.int32, shape, len(shape) - 1)


def rows_of(shape):
    return lax.broadcasted_iota(jnp.int32, shape, len(shape) - 2)


def low_half(x):
    return jnp.where(lanes_of(x.shape) < 64, x, pltpu.roll(x, 64, 1))


def high_half(x):
    return jnp.where(lanes_of(x.shape) < 64, pltpu.roll(x, 64, 1), x)


def unpack_tables(cos_ref, sin_ref):
    c, s = cos_ref[...], sin_ref[...]
    cos = jnp.concatenate([low_half(c), high_half(c)], axis=0)
    sin = jnp.concatenate([low_half(s), high_half(s)], axis=0)
    sin = jnp.where(lanes_of(sin.shape) < 64, -sin, sin)
    return cos, sin


def rot(x, cos, sin):
    return x * cos + pltpu.roll(x, 64, 1) * sin


def spread(row):
    parts = []
    for i in range(row.shape[0]):
        parts.append(jnp.broadcast_to(row[i : i + 1, :], (128, 128)).T)
    return jnp.concatenate(parts, axis=0)


def compact(x):
    eye = rows_of((128, 128)) == lanes_of((128, 128))
    parts = []
    for i in range(x.shape[0] // 128):
        block = x[i * 128 : (i + 1) * 128, :]
        parts.append(jnp.sum(jnp.where(eye, block, 0.0), axis=0, keepdims=True))
    return jnp.concatenate(parts, axis=0)


def row_sum(x):
    return jnp.broadcast_to(jnp.sum(x, axis=1, keepdims=True), x.shape)


def prep_kernel(info, k_ref, v_ref, cos_ref, sin_ref, kr_ref, send_ref, rows_ref):
    g = pl.program_id(0)
    tok = k_ref.shape[1]
    nb = rows_ref.shape[2]
    rate = tok // nb
    cos, sin = unpack_tables(cos_ref, sin_ref)
    for hh in range(2):
        h = 2 * g + hh
        hot = (lanes_of((nb, tok)) == info[4 + h] + rate * rows_of((nb, tok))).astype(bf16)
        kr = rot(k_ref[h].astype(f32), cos, sin).astype(bf16)
        kr_ref[h] = kr
        rows_ref[0, hh] = dot_nn(hot, kr).astype(bf16)
        rows_ref[1, hh] = dot_nn(hot, v_ref[h]).astype(bf16)
    par = info[1]
    send_ref[0, 0] = kr_ref[2 * g + par]
    send_ref[1, 0] = v_ref[2 * g + par]


def make_own_kernel(first, aliased):
    def own_kernel(info, start_ref, q_ref, k_ref, v_ref, cos_ref, sin_ref, *refs):
        refs = refs[aliased:]
        qr_ref, qt_ref, e_ref, acc_ref, m_ref, l_ref, rows_ref, bias_ref = refs
        tok = q_ref.shape[1]
        nb = rows_ref.shape[1]
        rate = tok // nb
        half = tok // 2
        scale = 1.0 / math.sqrt(q_ref.shape[2])

        @pl.when(pl.program_id(0) == 0)
        def _():
            start = spread(start_ref[...])
            for c in range(tok // 128):
                key = lanes_of((tok, 128)) + c * 128
                ok = (key <= rows_of((tok, 128))) & (key.astype(f32) >= start)
                bias_ref[:, c * 128 : (c + 1) * 128] = jnp.where(ok, 0.0, NEG)

        cos, sin = unpack_tables(cos_ref, sin_ref)
        for hh in range(2):
            h = 2 * (pl.program_id(0) + first) + hh
            q = rot(q_ref[hh].astype(f32), cos, sin).astype(bf16)
            qr_ref[h] = q
            qt_ref[h] = q.T
            hot = (lanes_of((nb, tok)) == info[4 + h] + rate * rows_of((nb, tok))).astype(bf16)
            rows_ref[hh] = dot_nn(hot, q).astype(bf16)
            vals = jnp.concatenate([v_ref[h], jnp.ones((tok, 128), bf16)], axis=1)
            for c in range(2):
                lo, n = c * half, (c + 1) * half
                z = dot_nt(q[lo:n], k_ref[h, :n, :]) * scale + bias_ref[lo:n, :n]
                m = jnp.max(z, axis=1, keepdims=True)
                e = jnp.exp(z - m).astype(bf16)
                e_ref[h, lo:n, :n] = e
                out = dot_nn(e, vals[:n])
                acc_ref[h, lo:n, :] = out[:, :128]
                l_ref[h, lo:n, :] = out[:, 128:]
                m_ref[h, lo:n, :] = jnp.broadcast_to(m, (half, 128))

    return own_kernel


def split3(x):
    hi = x.astype(bf16).astype(f32)
    mid = (x - hi).astype(bf16).astype(f32)
    return hi, mid, x - hi - mid


def pack3(parts, rows):
    stack = [p for x in parts for p in split3(x)]
    used = sum(p.shape[0] for p in stack)
    if used < rows:
        stack.append(jnp.zeros((rows - used, 128), f32))
    return jnp.concatenate(stack, axis=0).astype(bf16)


def unpack3(block, n, which):
    x = block.astype(f32)
    i = 3 * n * which
    return x[i : i + n] + x[i + n : i + 2 * n] + x[i + 2 * n : i + 3 * n]


def next_kernel(info, start_ref, q_ref, k_ref, v_ref, cos_ref, sin_ref, o_ref, e_ref, qn_ref, bias_ref, m_s, l_s):
    g = pl.program_id(0)
    tok = q_ref.shape[1]
    half = tok // 2
    scale = 1.0 / math.sqrt(q_ref.shape[2])
    h = 2 * g + info[1]

    @pl.when(g == 0)
    def _():
        start = spread(start_ref[...])
        for c in range(tok // 128):
            key = (lanes_of((tok, 128)) + c * 128).astype(f32)
            bias_ref[:, c * 128 : (c + 1) * 128] = jnp.where(key >= start, 0.0, NEG)

    cos, sin = unpack_tables(cos_ref, sin_ref)
    q = rot(q_ref[0].astype(f32), cos, sin).astype(bf16)
    qn_ref[g] = q.T
    vals = jnp.concatenate([v_ref[h], jnp.ones((tok, 128), bf16)], axis=1)
    for c in range(2):
        sl = slice(c * half, (c + 1) * half)
        z = dot_nt(q[sl], k_ref[h]) * scale + bias_ref[sl, :]
        m = jnp.max(z, axis=1, keepdims=True)
        e = jnp.exp(z - m).astype(bf16)
        e_ref[g, sl, :] = e
        out = dot_nn(e, vals)
        o_ref[0, sl, :] = out[:, :128].astype(bf16)
        m_s[sl, :] = jnp.broadcast_to(m, (half, 128))
        l_s[sl, :] = out[:, 128:]
    o_ref[0, tok:, :] = pack3((compact(m_s[...]), compact(l_s[...])), o_ref.shape[1] - tok)


def key_order(index, codes, nb, part, count):
    col = lanes_of((1, count)) + part * count
    slot = col // nb
    dev = jnp.full((1, count), index, jnp.int32)
    for b, code in enumerate(codes):
        dev = dev ^ (((slot >> b) & 1) * code)
    return dev * nb + col % nb


def make_join_kernel(codes):
    def join_kernel(
        info, start_ref, acc_ref, m_ref, l_ref, on_ref, q1_ref, ga_ref, gb_ref, og_ref, gain_ref,
        attn_ref, rr_ref, ls_ref, e1_ref, rs_ref, ar_ref, or_ref, stat_ref,
        start_s, m_s, l_s, acc_s, sq_s, cr_s,
    ):
        g = pl.program_id(0)
        index, sel = info[0], info[2]
        tok = og_ref.shape[1]
        nb = q1_ref.shape[1]
        rate = tok // nb
        count = ga_ref.shape[2]
        scale = 1.0 / math.sqrt(og_ref.shape[2])

        @pl.when(g == 0)
        def _():
            start_s[...] = spread(start_ref[...])
            sq_s[...] = jnp.zeros_like(sq_s)
            cr_s[...] = jnp.zeros_like(cr_s)

        stats = on_ref[0, tok:, :]
        n = tok // 128
        ok = index > 0
        m_prev = jnp.where(ok, spread(unpack3(stats, n, 0)), NEG)
        l_prev = spread(unpack3(stats, n, 1))
        m_own = m_ref[2 * g + sel]
        mn = jnp.maximum(m_own, m_prev)
        a_own = jnp.exp(m_own - mn)
        a_prev = jnp.where(ok, jnp.exp(m_prev - mn), 0.0)
        m_s[sel] = mn
        l_s[sel] = a_own * l_ref[2 * g + sel] + a_prev * l_prev
        acc_s[sel] = a_own * acc_ref[2 * g + sel] + a_prev * on_ref[0, :tok, :].astype(f32)
        m_s[1 - sel] = m_ref[2 * g + 1 - sel]
        l_s[1 - sel] = l_ref[2 * g + 1 - sel]
        acc_s[1 - sel] = acc_ref[2 * g + 1 - sel]

        for hh in range(2):
            h = 2 * g + hh
            off = info[4 + h]
            rows = pl.ds(off, nb, stride=rate)
            here = sel == hh
            m_own = m_ref[h]

            q1 = q1_ref[hh]
            start1 = start_s[rows, :][:, :1]
            qb = index * nb + rows_of((nb, count))
            zs = []
            for part, ref in enumerate((ga_ref, gb_ref)):
                kb = key_order(index, codes, nb, part, count)
                pos = (off + rate * kb - index * tok).astype(f32)
                ok = (kb <= qb) & (pos >= start1)
                zs.append(jnp.where(ok, dot_nt(q1, ref[0, hh]) * scale, NEG))
            m1 = jnp.maximum(jnp.max(zs[0], axis=1, keepdims=True), jnp.max(zs[1], axis=1, keepdims=True))
            o1 = jnp.zeros((nb, 256), f32)
            for part, ref in enumerate((ga_ref, gb_ref)):
                e1 = jnp.exp(zs[part] - m1).astype(bf16)
                e1_ref[hh, :, part * count : (part + 1) * count] = e1
                v1 = jnp.concatenate([ref[1, hh], jnp.ones((count, 128), bf16)], axis=1)
                o1 = o1 + dot_nn(e1, v1)

            mr = m_s[hh, rows, :]
            lr = l_s[hh, rows, :]
            ar = acc_s[hh, rows, :]
            m1b = jnp.broadcast_to(m1, (nb, 128))
            mn = jnp.maximum(mr, m1b)
            b0 = jnp.exp(mr - mn)
            b1 = jnp.exp(m1b - mn)
            ln = b0 * lr + b1 * o1[:, 128:]
            m_s[hh, rows, :] = mn
            l_s[hh, rows, :] = ln
            acc_s[hh, rows, :] = b0 * ar + b1 * o1[:, :128]
            lse1 = mn + jnp.log(ln)
            rs_ref[hh] = jnp.where(lanes_of((nb, 128)) < 64, lse1, b1 / ln)

            inv = 1.0 / l_s[hh]
            attn = (acc_s[hh] * inv).astype(bf16)
            attn_ref[h] = attn
            both = jnp.where((lanes_of((tok, 128)) < 64) | jnp.logical_not(here), m_own, m_prev)
            rr_ref[h] = jnp.exp(both - m_s[hh]) * inv
            af = attn.astype(f32)
            gd = og_ref[hh].astype(f32) * gain_ref[hh]
            sq_s[...] += af * af
            cr_s[...] += gd * af
            hot = (lanes_of((nb, tok)) == off + rate * rows_of((nb, tok))).astype(bf16)
            ar_ref[hh] = dot_nn(hot, attn).astype(bf16)
            or_ref[hh] = dot_nn(hot, og_ref[hh]).astype(bf16)

        ls_ref[g] = m_s[sel] + jnp.log(l_s[sel])

        @pl.when(g == pl.num_programs(0) - 1)
        def _():
            stat_ref[...] = jnp.concatenate([compact(row_sum(sq_s[...])), compact(row_sum(cr_s[...]))], axis=0)

    return join_kernel


def norm_terms(stat_ref, other_ref, feats):
    total = stat_ref[...] + other_ref[...]
    n = total.shape[0] // 2
    rinv = lax.rsqrt(total[:n] / feats + eps_norm)
    return rinv, rinv * rinv * total[n:] / feats


def split3(x):
    hi = x.astype(bf16).astype(f32)
    mid = (x - hi).astype(bf16).astype(f32)
    return hi, mid, x - hi - mid


def grad_terms(attn, og, gain, rinv, cc):
    af = attn.astype(f32)
    gd = og.astype(f32) * gain
    ag = (rinv * (gd - af * cc)).astype(bf16).astype(f32)
    return af, ag, row_sum(ag * af)


def make_rows_kernel(feats):
    def rows_kernel(
        info, begin_ref, stat_ref, other_ref, ar_ref, or_ref, q1_ref, gain_ref, rs_ref, attn_ref, rr_ref, og_ref,
        out_ref, st_ref, do_ref, rinv_s, cc_s, st_s,
    ):
        g = pl.program_id(0)
        sel = info[2]
        nb = ar_ref.shape[1]
        tok = og_ref.shape[1]
        rate = tok // nb

        @pl.when(g == 0)
        def _():
            rinv, cc = norm_terms(stat_ref, other_ref, feats)
            rinv_s[...] = spread(rinv)
            cc_s[...] = spread(cc)
            st_s[...] = spread(begin_ref[...])
            st_ref[...] = jnp.zeros_like(st_ref)

        for hh in range(2):
            rows = pl.ds(info[4 + 2 * g + hh], nb, stride=rate)
            af = ar_ref[hh].astype(f32)
            gd = or_ref[hh].astype(f32) * gain_ref[hh]
            ag = (rinv_s[rows, :] * (gd - af * cc_s[rows, :])).astype(bf16)
            delta = row_sum(ag.astype(f32) * af)
            out_ref[0, hh] = ag
            lane = lanes_of((nb, 128))
            spot = lane == (2 * g + hh) * nb + rows_of((nb, 128))
            for i, x in enumerate(split3(low_half(rs_ref[hh])) + split3(delta) + split3(st_s[rows, :])):
                st_ref[i : i + 1, :] += jnp.sum(jnp.where(spot, x, 0.0), axis=0, keepdims=True)
            out_ref[1, hh] = q1_ref[hh]

        h = 2 * g + sel
        af, ag, delta = grad_terms(attn_ref[h], og_ref[0], gain_ref[sel], rinv_s[...], cc_s[...])
        r = high_half(rr_ref[h])
        do_ref[0, :tok, :] = (ag * r).astype(bf16)
        do_ref[0, tok:, :] = pack3((compact(delta * r),), do_ref.shape[1] - tok)

    return rows_kernel


def next_back_kernel(info, do_ref, q_ref, v_ref, e_ref, dk_ref, dv_ref):
    g = pl.program_id(0)
    h = 2 * g + info[1]
    tok = e_ref.shape[1]
    half = tok // 2
    dl = spread(unpack3(do_ref[0, tok:, :], tok // 128, 0))
    dk = jnp.zeros((128, tok), f32)
    dv = jnp.zeros((128, tok), f32)
    for c in range(2):
        sl = slice(c * half, (c + 1) * half)
        e = e_ref[g, sl, :]
        do = do_ref[0, sl, :]
        dp = dot_nt(do, v_ref[h])
        ds = (e.astype(f32) * (dp - jnp.concatenate([dl[sl]] * (tok // 128), axis=1))).astype(bf16)
        dk = dk + dot_nn(q_ref[g, :, sl], ds)
        dv = dv + dot_tn(do, e)
    dk_ref[g] = dk.T
    dv_ref[g] = dv.T


def make_prev_back_kernel(feats):
    def prev_back_kernel(
        info, start_ref, stat_ref, other_ref, q_ref, attn_ref, ls_ref, og_ref, gain_ref, kv_ref,
        dq_ref, bias_ref, rinv_s, cc_s,
    ):
        g = pl.program_id(0)
        index, sel = info[0], info[2]
        tok = q_ref.shape[1]
        half = tok // 2
        scale = 1.0 / math.sqrt(q_ref.shape[2])
        h = 2 * g + sel

        @pl.when(g == 0)
        def _():
            rinv, cc = norm_terms(stat_ref, other_ref, feats)
            rinv_s[...] = spread(rinv)
            cc_s[...] = spread(cc)
            start = spread(start_ref[...])
            first = jnp.where(index == 0, float(tok), 0.0)
            for c in range(tok // 128):
                key = (lanes_of((tok, 128)) + c * 128).astype(f32)
                ok = (key - tok >= start) & (key >= first)
                bias_ref[:, c * 128 : (c + 1) * 128] = jnp.where(ok, 0.0, NEG)

        af, ag, delta = grad_terms(attn_ref[h], og_ref[0], gain_ref[0], rinv_s[...], cc_s[...])
        do = ag.astype(bf16)
        lse = ls_ref[g]
        for c in range(2):
            sl = slice(c * half, (c + 1) * half)
            wide = lambda x: jnp.concatenate([x[sl]] * (tok // 128), axis=1)
            z = dot_nt(q_ref[h, sl, :], kv_ref[0, 0]) * scale + bias_ref[sl, :]
            prob = jnp.exp(z - wide(lse)).astype(bf16)
            dp = dot_nt(do[sl], kv_ref[1, 0])
            ds = (prob.astype(f32) * (dp - wide(delta))).astype(bf16)
            dq_ref[g, sl, :] = dot_nn(ds, kv_ref[0, 0])

    return prev_back_kernel


def make_back_own_kernel(feats, first, aliased):
    def back_own_kernel(
        info, stat_ref, other_ref, q_ref, k_ref, v_ref, attn_ref, rr_ref, e_ref,
        og_ref, gain_ref, e1_ref, rs_ref, ga_ref, gb_ref, *refs
    ):
        normed_ref, dq_ref, dk_ref, dv_ref, rinv_s, cc_s, ag_s, de_s = refs[aliased:]
        step = pl.program_id(0)
        tok = og_ref.shape[1]
        nb = e1_ref.shape[1]
        rate = tok // nb
        count = ga_ref.shape[2]
        half = tok // 2

        @pl.when(step == 0)
        def _():
            rinv, cc = norm_terms(stat_ref, other_ref, feats)
            rinv_s[...] = spread(rinv)
            cc_s[...] = spread(cc)

        for hh in range(2):
            h = 2 * (step + first) + hh
            rinv = rinv_s[...]
            af, ag, delta = grad_terms(attn_ref[h], og_ref[hh], gain_ref[hh], rinv, cc_s[...])
            normed_ref[hh] = (af * rinv * gain_ref[hh]).astype(bf16)
            ag_s[hh] = ag
            de_s[hh] = delta
            r = low_half(rr_ref[h])
            do = (ag * r).astype(bf16)
            dl = delta * r
            dks = []
            for c in range(2):
                lo, n = c * half, (c + 1) * half
                sl = slice(lo, n)
                e = e_ref[h, sl, :n]
                dp = dot_nt(do[sl], v_ref[h, :n, :])
                ds = (e.astype(f32) * (dp - jnp.concatenate([dl[sl]] * (n // 128), axis=1))).astype(bf16)
                dq_ref[h, sl, :] = dot_nn(ds, k_ref[h, :n, :])
                dks.append((dot_nn(q_ref[h, :, sl], ds), dot_tn(do[sl], e)))
            for i, ref in enumerate((dk_ref, dv_ref)):
                ref[h, :half, :] = (dks[0][i] + dks[1][i][:, :half]).T
                ref[h, half:, :] = dks[1][i][:, half:].T

            rows = pl.ds(info[4 + h], nb, stride=rate)
            r1 = high_half(rs_ref[hh])
            g1 = (ag_s[hh, rows, :] * r1).astype(bf16)
            d1 = (de_s[hh, rows, :] * r1)[:, :1]
            dq1 = jnp.zeros((nb, 128), f32)
            for part, ref in enumerate((ga_ref, gb_ref)):
                dp1 = dot_nt(g1, ref[1, hh])
                ds1 = (e1_ref[hh, :, part * count : (part + 1) * count].astype(f32) * (dp1 - d1)).astype(bf16)
                dq1 = dq1 + dot_nn(ds1, ref[0, hh])
            dq_ref[h, rows, :] += dq1

    return back_own_kernel


def make_final_kernel(codes):
    def final_kernel(
        info, dq_ref, dk_ref, dv_ref, dkn_ref, dvn_ref, dqn_ref, rows_ref, sa_ref, sb_ref, ta_ref, tb_ref, cos_ref, sin_ref,
        gq_ref, gk_ref, gv_ref, dk_s, dv_s,
    ):
        g = pl.program_id(0)
        index, par, sel = info[0], info[1], info[2]
        tok = dk_ref.shape[1]
        nb = rows_ref.shape[2]
        rate = tok // nb
        count = sa_ref.shape[2]
        scale = 1.0 / math.sqrt(dk_ref.shape[2])
        cos, sin = unpack_tables(cos_ref, sin_ref)
        kb = index * nb + rows_of((nb, count))
        slots = ta_ref.shape[0]
        keep = rows_of((slots * 16, count)) // 16 == lanes_of((slots * 16, count)) // nb
        fold = (rows_of((16, slots * 16)) == lanes_of((16, slots * 16)) % 16).astype(bf16)
        for hh in range(2):
            h = 2 * g + hh
            off = info[4 + h]
            dq = dq_ref[h] * scale + jnp.where(sel == hh, dqn_ref[g] * scale, 0.0)
            gq_ref[hh] = rot(dq, cos, -sin).astype(bf16)
            here = par == hh
            dk_s[hh] = (dk_ref[h] + jnp.where(here, dkn_ref[g], 0.0)) * scale
            dv_s[hh] = dv_ref[h] + jnp.where(here, dvn_ref[g], 0.0)
            k1 = rows_ref[0, hh]
            v1 = rows_ref[1, hh]
            kpos = (off + rate * kb).astype(f32)
            dk1 = jnp.zeros((nb, 128), f32)
            dv1 = jnp.zeros((nb, 128), f32)
            pick = (rows_of((128, count)) == h * nb + lanes_of((128, count)) % nb).astype(bf16)
            for part, (s, t) in enumerate(((sa_ref, ta_ref), (sb_ref, tb_ref))):
                qb = key_order(index, codes, nb, part, count)
                each = dot_nn(t[...].reshape(slots * 16, 128), pick)
                st = dot_nn(fold, jnp.where(keep, each, 0.0).astype(bf16))
                lse = st[0:1] + st[1:2] + st[2:3]
                delta = st[3:4] + st[4:5] + st[5:6]
                start = st[6:7] + st[7:8] + st[8:9]
                ok = (kb <= qb) & (kpos >= start)
                z = jnp.where(ok, dot_nt(k1, s[1, hh]) * scale - lse, NEG)
                p = jnp.exp(z).astype(bf16)
                dp = dot_nt(v1, s[0, hh])
                ds = (p.astype(f32) * (dp - delta)).astype(bf16)
                dk1 = dk1 + dot_nn(ds, s[1, hh])
                dv1 = dv1 + dot_nn(p, s[0, hh])
            rows = pl.ds(off, nb, stride=rate)
            dk_s[hh, rows, :] += dk1 * scale
            dv_s[hh, rows, :] += dv1
            gk_ref[hh] = rot(dk_s[hh], cos, -sin).astype(bf16)
            gv_ref[hh] = dv_s[hh].astype(bf16)

    return final_kernel


def call(kernel, prefetch, grid, ins, outs, scratch=(), alias=(), cost=None):
    arrays, in_specs = [], []
    for a, b, m in ins:
        if b is None:
            arrays.append(pltpu.with_memory_space_constraint(a, pltpu.VMEM))
            in_specs.append(pl.BlockSpec(memory_space=pltpu.VMEM))
        else:
            arrays.append(a)
            in_specs.append(pl.BlockSpec(b, m))
    out_shape, out_specs = [], []
    for s, d, b, m in outs:
        if b is None:
            out_shape.append(pltpu.VMEM(s, d))
            out_specs.append(pl.BlockSpec(memory_space=pltpu.VMEM))
        else:
            out_shape.append(jax.ShapeDtypeStruct(s, d))
            out_specs.append(pl.BlockSpec(b, m))
    us = 4
    return pl.pallas_call(
        kernel,
        out_shape=out_shape,
        grid_spec=pltpu.PrefetchScalarGridSpec(
            num_scalar_prefetch=len(prefetch),
            grid=grid,
            in_specs=in_specs,
            out_specs=out_specs,
            scratch_shapes=list(scratch),
        ),
        input_output_aliases={len(prefetch) + i: o for i, o in alias},
        cost_estimate=pl.CostEstimate(flops=0, transcendentals=0, bytes_accessed=int(us * 3.0e6)),
        compiler_params=pltpu.CompilerParams(
            dimension_semantics=("arbitrary",) * len(grid), vmem_limit_bytes=24 << 20
        ),
    )(*prefetch, *arrays)


def after(x, *deps):
    return lax.optimization_barrier((x, *deps))[0]


def body(queries, keys, values, out_grad, norm_gain, doc_start, head_offsets):
    heads, tok, width = queries.shape
    ctx = lax.axis_size("ctx")
    rate = ctx * tok // SEL
    nb = tok // rate
    feats = float(HEADS * width)
    pairs = heads // 2
    index = lax.axis_index("ctx")
    base = index * tok
    codes = [1 << b for b in range(2, ctx.bit_length() - 1)] + [2, 1]

    starts = lax.dynamic_slice_in_dim(doc_start, base, tok)
    position = base + jnp.arange(tok, dtype=jnp.int32)
    rel = (position - starts).astype(f32)
    freq = theta_base ** (-2.0 * jnp.arange(width // 2).astype(f32) / width)

    def tables(rel):
        angle = jnp.concatenate([rel[: tok // 2, None] * freq, rel[tok // 2 :, None] * freq], axis=1)
        return jnp.cos(angle), jnp.sin(angle)

    cos, sin = tables(rel)
    begin = starts.astype(f32).reshape(tok // 128, 128)
    after_starts = lax.dynamic_slice_in_dim(doc_start, jnp.minimum(base + tok, (ctx - 1) * tok), tok)
    next_start = (after_starts - base).astype(f32).reshape(tok // 128, 128)
    rel_next = (position + tok - after_starts).astype(f32)
    cos_next, sin_next = tables(rel_next)
    start_rel = (starts - base).astype(f32).reshape(tok // 128, 128)
    spot = jnp.arange(4 + heads, dtype=jnp.int32)
    info = jnp.pad(head_offsets, (4, 0)).astype(jnp.int32)
    info = info + jnp.where(spot == 0, index, 0) + jnp.where(spot == 1, index % 2, 0) + jnp.where(spot == 2, (index + 1) % 2, 0)
    gain = norm_gain.reshape(heads, 1, width)

    pair3 = (2, tok, width)
    one3 = (1, tok, width)
    full = queries.shape
    const = lambda n: (lambda i, *s: (0,) * n)
    whole = lambda a: (a, a.shape, const(a.ndim))
    vm = lambda a: (a, None, None)
    hbm = lambda a: pltpu.with_memory_space_constraint(a, pltpu.HBM)
    gp = lambda g, *s: (g, 0, 0)
    g4 = lambda g, *s: (0, g, 0, 0)

    def swap(x, code):
        return lax.ppermute(x, "ctx", [(i, i ^ code) for i in range(ctx)])

    half_count = SEL // 2

    up = [(i, i + 1) for i in range(ctx - 1)]
    down = [(i + 1, i) for i in range(ctx - 1)]
    mine = lambda g, s, *_: (2 * g + s[2], 0, 0)
    lead, z_code, y_code, core = codes[:-3], codes[-3], codes[-2], codes[-1]

    def join2(x, code, *deps):
        y = swap(x, code)
        return jnp.concatenate([x, after(y, *deps) if deps else y], axis=2)

    q_send = lax.dynamic_index_in_dim(queries.reshape(pairs, 2, tok, width), (index + 1) % 2, 1, keepdims=False)
    q_raw = lax.ppermute(q_send, "ctx", down)
    k_rot, kv_send, rows = call(
        prep_kernel, (info,), (pairs,),
        [vm(keys), vm(values), whole(cos), whole(sin)],
        [
            (full, bf16, None, None),
            ((2, pairs, tok, width), bf16, (2, 1, tok, width), g4),
            ((2, heads, nb, width), bf16, (2, 2, nb, width), g4),
        ],
    )
    vals = values
    x = rows
    for code in lead[:-1]:
        x = join2(x, code)
    ahead = [swap(x, code) for code in lead[-1:]]

    def own(first, n, qs, prior):
        outs = [
            (full, bf16, None, None),
            ((heads, width, tok), bf16, None, None),
            ((heads, tok, tok), bf16, None, None),
            (full, f32, None, None),
            (full, f32, None, None),
            (full, f32, None, None),
            ((heads, nb, width), bf16, (2, nb, width), lambda g, *s: (g + first, 0, 0)),
        ]
        ins = [
            whole(start_rel),
            (qs, pair3, lambda g, *s: (g + first, 0, 0)),
            vm(k_rot), vm(vals), whole(cos), whole(sin),
        ]
        alias = []
        for i, a in enumerate(prior):
            alias.append((len(ins), i))
            ins.append(vm(a) if i < 6 else (a, (2, nb, width), lambda g, *s: (first, 0, 0)))
        return call(
            make_own_kernel(first, len(prior)), (info,), (n,), ins, outs,
            [pltpu.VMEM((tok, tok), f32)], alias,
        )

    cut = pairs // 2
    part = own(0, cut, queries, [])
    for a in ahead:
        x = jnp.concatenate([x, after(a, part[3])], axis=2)
    x = after(x, part[3])
    pending = swap(x, z_code)
    extra = -(-6 * (tok // 128) // 16) * 16
    o_send, e_next, q_next = call(
        next_kernel, (info,), (pairs,),
        [
            whole(next_start),
            (after(q_raw, x), one3, gp),
            vm(k_rot), vm(vals), whole(cos_next), whole(sin_next),
        ],
        [
            ((pairs, tok + extra, width), bf16, (1, tok + extra, width), gp),
            ((pairs, tok, tok), bf16, None, None),
            ((pairs, width, tok), bf16, None, None),
        ],
        [pltpu.VMEM((tok, tok), f32)] + [pltpu.VMEM((tok, 128), f32)] * 2,
    )
    y = jnp.concatenate([x, after(pending, e_next)], axis=2)
    pending = swap(y, y_code)
    o_prev = lax.ppermute(o_send, "ctx", up)
    q_rot, q_t, e_own, acc, m_own, lsum, q1 = own(cut, pairs - cut, after(queries, y), part)
    ga = jnp.concatenate([y, after(pending, m_own)], axis=2)
    gb = swap(ga, core)
    kv_prev = lax.ppermute(after(kv_send, gb, o_prev), "ctx", up)

    attn, rr, lse, e1, rs, attn_rows, og_rows, stat = call(
        make_join_kernel(codes), (info,), (pairs,),
        [
            whole(start_rel), vm(acc), vm(m_own), vm(lsum),
            (o_prev, (1, tok + extra, width), gp),
            (q1, (2, nb, width), gp),
            (ga, (2, 2, half_count, width), g4),
            (gb, (2, 2, half_count, width), g4),
            (out_grad, pair3, gp),
            (gain, (2, 1, width), gp),
        ],
        [
            (full, bf16, None, None),
            (full, f32, None, None),
            ((pairs, tok, width), f32, None, None),
            ((heads, nb, SEL), bf16, (2, nb, SEL), gp),
            ((heads, nb, width), f32, (2, nb, width), gp),
            ((heads, nb, width), bf16, (2, nb, width), gp),
            ((heads, nb, width), bf16, (2, nb, width), gp),
            ((2 * tok // 128, 128), f32, (2 * tok // 128, 128), const(2)),
        ],
        [pltpu.VMEM((tok, 128), f32)] + [pltpu.VMEM((2, tok, 128), f32)] * 3 + [pltpu.VMEM((tok, 128), f32)] * 2,
    )
    other = lax.ppermute(stat, "head", [(0, 1), (1, 0)])

    more = -(-3 * (tok // 128) // 16) * 16
    rows1, stats1, do_send = call(
        make_rows_kernel(feats), (info,), (pairs,),
        [
            whole(begin), whole(stat), whole(other),
            (attn_rows, (2, nb, width), gp),
            (og_rows, (2, nb, width), gp),
            (q1, (2, nb, width), gp),
            (gain, (2, 1, width), gp),
            (rs, (2, nb, width), gp),
            vm(attn), vm(rr),
            (out_grad, one3, mine),
        ],
        [
            ((2, heads, nb, width), bf16, (2, 2, nb, width), g4),
            ((16, 128), f32, (16, 128), const(2)),
            ((pairs, tok + more, width), bf16, (1, tok + more, width), gp),
        ],
        [pltpu.VMEM((tok, 128), f32)] * 3,
    )
    flat = jnp.concatenate([rows1.reshape(2 * heads * nb, width), stats1.astype(bf16)], axis=0)[None]

    def join0(x, y):
        return jnp.concatenate([x, y], axis=0)

    x = flat
    for code in lead[:-1]:
        x = join0(x, swap(x, code))
    ahead = [swap(x, code) for code in lead[-1:]]
    do_next = lax.ppermute(do_send, "ctx", down)

    def back_own(first, n, deps, prior):
        hp = lambda h, *s: (h + first, 0, 0)
        hg = lambda h, *s: (0, h + first, 0, 0)
        ins = [
            whole(stat), whole(after(other, *deps)),
            vm(q_t), vm(k_rot), vm(vals), vm(attn), vm(rr), vm(e_own),
            (out_grad, pair3, hp),
            (gain, (2, 1, width), hp),
            (e1, (2, nb, SEL), hp),
            (rs, (2, nb, width), hp),
            (ga, (2, 2, half_count, width), hg),
            (gb, (2, 2, half_count, width), hg),
        ]
        alias = []
        for i, a in enumerate(prior):
            alias.append((len(ins), i))
            ins.append(vm(a) if i >= 1 else (a, (1, 16, width), lambda h, *s: (2 * first, 0, 0)))
        return call(
            make_back_own_kernel(feats, first, len(prior)), (info,), (n,), ins,
            [
                (full, bf16, pair3, hp),
                (full, f32, None, None),
                (full, f32, None, None),
                (full, f32, None, None),
            ],
            [pltpu.VMEM((tok, 128), f32)] * 2 + [pltpu.VMEM((2, tok, 128), f32)] * 2,
            alias,
        )

    part = back_own(0, cut, (flat, kv_prev), [])
    for a in ahead:
        x = join0(x, after(a, part[2]))
    x = after(x, part[2])
    pending = swap(x, z_code)
    normed, dq_own, dk_own, dv_own = back_own(cut, pairs - cut, (x,), part)
    y = join0(x, after(pending, dk_own))
    pending = swap(y, y_code)

    dk_next, dv_next = call(
        next_back_kernel, (info,), (pairs,),
        [
            (after(do_next, y), (1, tok + more, width), gp),
            vm(q_next), vm(vals), vm(e_next),
        ],
        [
            ((pairs, tok, width), f32, None, None),
            ((pairs, tok, width), f32, None, None),
        ],
    )
    (dq_prev,) = call(
        make_prev_back_kernel(feats), (info,), (pairs,),
        [
            whole(after(start_rel, dk_next)), whole(stat), whole(other),
            vm(q_rot), vm(attn), vm(lse),
            (out_grad, one3, mine),
            (gain, (1, 1, width), mine),
            (kv_prev, (2, 1, tok, width), g4),
        ],
        [((pairs, tok, width), f32, None, None)],
        [pltpu.VMEM((tok, tok), f32)] + [pltpu.VMEM((tok, 128), f32)] * 2,
    )
    sa = join0(y, after(pending, dq_prev))
    sb = swap(sa, core)

    def sort(x):
        slots = x.shape[0]
        near = x[:, : 2 * heads * nb].reshape(slots, 2, heads, nb, width)
        near = near.transpose(1, 2, 0, 3, 4).reshape(2, heads, slots * nb, width)
        return near, x[:, 2 * heads * nb :]

    (sa, ta), (sb, tb) = sort(sa), sort(sb)
    grad_queries, grad_keys, grad_values = call(
        make_final_kernel(codes), (info,), (pairs,),
        [
            vm(dq_own), vm(dk_own), vm(dv_own), vm(dk_next), vm(dv_next), vm(dq_prev),
            (rows, (2, 2, nb, width), g4),
            (sa, (2, 2, half_count, width), g4),
            (sb, (2, 2, half_count, width), g4),
            whole(ta), whole(tb),
            whole(cos), whole(sin),
        ],
        [
            (full, bf16, pair3, gp),
            (full, bf16, pair3, gp),
            (full, bf16, pair3, gp),
        ],
        [pltpu.VMEM((2, tok, 128), f32)] * 2,
    )
    return (normed, grad_queries, grad_keys, grad_values)


def solution(mesh):
    return jax.shard_map(
        body,
        mesh=mesh,
        in_specs=(
            P("head", "ctx", None),
            P("head", "ctx", None),
            P("head", "ctx", None),
            P("head", "ctx", None),
            P("head", None),
            P(),
            P("head"),
        ),
        out_specs=(
            P("head", "ctx", None),
            P("head", "ctx", None),
            P("head", "ctx", None),
            P("head", "ctx", None),
        ),
        check_vma=False,
    )
```
